32 devices in a mesh: seg: 4 (over y, x), gx: 2 (over core), gy: 4 (over z).
Axes of the slice: x: 2, y: 2, z: 4, core: 2. Of those that a mesh axis runs over, the one named last changes fastest.
Arguments:
- gas_state: float32 [7, 384, 32, 512], P(None, 'seg', 'gx', 'gy'), may hold values from 0 to 1
- solids_temp: float32 [384, 32, 512], P('seg', 'gx', 'gy'), may hold values from 0.2 to 1.2
- exchange_rate: float32 [32, 512], P('gx', 'gy'), may hold values from 0.1 to 0.5
- column_flags: int32 [32, 512], P('gx', 'gy'), may hold values from 0 to 3
- block_inverse: float32 [384, 96], P('seg'), may hold values from -1 to 2, as said below
- line_coupling: float32 [4, 2], P('seg'), may hold values from 0.05 to 0.25
Outputs:
- gas_next: float32 [7, 384, 32, 512], P(None, 'seg', 'gx', 'gy')
- solids_next: float32 [384, 32, 512], P('seg', 'gx', 'gy')
The draws below stay inside these ranges and needn't reach their ends.
Inputs may be any that keep to these rules, and one draw needn't show every extreme that they name: `block_inverse`: each block of 96 rows holds the inverse of that segment's diagonal block.
All inputs are finite; a program needn't handle non-finite values.
Results may differ from the reference program's by a relative error of at most 0.000061.
Values sent between devices are 32-bit elements; how exact they have to be, the bound alone decides.
A program may use at most 192 MiB of HBM per device.

```python
import math
import jax
import jax.numpy as jnp
from jax import lax

NSP = 6
CZ = 96
NZ = 384
NX = 32
NY = 512
N_SEG = 4


def draw_block_inverse(key, part):
    noise_key, diag_key = jax.random.split(jax.random.fold_in(key, 7))
    spread = 0.45 / math.sqrt(CZ)
    offdiag = jnp.clip(jax.random.normal(noise_key, (NZ, CZ), jnp.float32), -3.0, 3.0) * spread
    diagonal = jax.random.uniform(diag_key, (NZ, CZ), jnp.float32, 1.5, 2.0)
    local_row = jnp.arange(NZ) % CZ
    on_diag = local_row[:, None] == jnp.arange(CZ)[None, :]
    return jnp.where(on_diag, diagonal, offdiag)


def plant(values, own_key, least, top_value):
    longest = values.shape.index(max(values.shape))
    spots = []
    for shift in (0, 1):
        where = [jax.random.randint(jax.random.fold_in(own_key, axis), (), 0, length) for axis, length in enumerate(values.shape)]
        where[longest] = (where[longest] + shift) % values.shape[longest]
        spots.append(tuple(where))
    return values.at[spots[0]].set(least).at[spots[1]].set(top_value)


def shard_levels(key, dims, shards, least, top_value):
    gain, own = 1.0, jax.random.fold_in(key, 6)
    for dim, blocks in shards:
        steps = jnp.exp(jax.random.uniform(jax.random.fold_in(own, dim), (blocks,), jnp.float32, least / len(shards), top_value / len(shards)))
        gain = gain * jnp.repeat(steps, dims[dim] // blocks).reshape([-1 if axis == dim else 1 for axis in range(len(dims))])
    return gain


def setup_inputs(seed: int = 0) -> dict:
    keys = jax.random.split(jax.random.key(seed), 7)
    return {
        "gas_state": jnp.clip(1.0 * jax.random.uniform(keys[0], (NSP + 1, NZ, NX, NY), jnp.float32) ** shard_levels(keys[0], (NSP + 1, NZ, NX, NY), ((1, 4), (2, 2), (3, 4)), -0.2, 0.2), 0.0, 1.0),
        "solids_temp": jnp.clip(0.2 + 1 * jax.random.uniform(keys[1], (NZ, NX, NY), jnp.float32) ** shard_levels(keys[1], (NZ, NX, NY), ((0, 4), (1, 2), (2, 4)), -0.2, 0.2), 0.2, 1.2),
        "exchange_rate": jnp.clip(jnp.exp(math.log(0.5) - 1.609438 * jax.random.uniform(keys[2], (NX, NY), jnp.float32) ** shard_levels(keys[2], (NX, NY), ((0, 2), (1, 4)), -0.2, 0.2)), 0.1, 0.5),
        "column_flags": plant(jax.random.randint(keys[3], (NX, NY), 0, 4), jax.random.fold_in(keys[3], 1), 0, 3).astype(jnp.int32),
        "block_inverse": draw_block_inverse(jax.random.fold_in(keys[6], 71), 0),
        "line_coupling": jnp.clip(0.05 + 0.2 * jax.random.uniform(keys[5], (N_SEG, 2), jnp.float32) ** shard_levels(keys[5], (N_SEG, 2), ((0, 4),), -0.2, 0.2), 0.05, 0.25),
    }


diffusion = (0.1, 0.08, 0.12, 0.09, 0.11, 0.07)
stoich = (-1.0, -0.5, 1.0, 0.5, 0.25, 0.75)
rate_const = 0.3
upwind = 0.25
cond_base = 0.04
cond_slope = 0.3
heat_release = 0.5
lateral = 0.1
loss_table = (0.0, 0.3, 0.0, 0.1)
feed_table = (0.0, 0.0, 0.4, 0.0)

def advance_species(padded, spread, gains, reaction):
    center = padded[:, 1:-1, 1:-1, 1:-1]
    beside = padded[:, 2:, 1:-1, 1:-1] + padded[:, :-2, 1:-1, 1:-1]
    beside = beside + padded[:, 1:-1, 2:, 1:-1] + padded[:, 1:-1, :-2, 1:-1]
    beside = beside + padded[:, 1:-1, 1:-1, 2:] + padded[:, 1:-1, 1:-1, :-2]
    below = padded[:, :-2, 1:-1, 1:-1]
    return center + spread * (beside - 6.0 * center) - upwind * (center - below) + gains * reaction[None]

def lookup(flags, table):
    result = jnp.zeros(flags.shape, jnp.float32)
    for value, entry in enumerate(table):
        result = result + jnp.where(flags == value, entry, 0.0)
    return result

def advance_enthalpy(heat_pad, mix_pad, reaction, flags):
    cond = cond_base + cond_slope * mix_pad
    heat_mid = heat_pad[1:-1, 1:-1, 1:-1]
    cond_mid = cond[1:-1, 1:-1, 1:-1]
    flux = jnp.zeros(heat_mid.shape, heat_mid.dtype)
    views = ((slice(2, None), slice(1, -1), slice(1, -1)), (slice(None, -2), slice(1, -1), slice(1, -1)), (slice(1, -1), slice(2, None), slice(1, -1)), (slice(1, -1), slice(None, -2), slice(1, -1)), (slice(1, -1), slice(1, -1), slice(2, None)), (slice(1, -1), slice(1, -1), slice(None, -2)))
    for view in views:
        flux = flux + 0.5 * (cond_mid + cond[view]) * (heat_pad[view] - heat_mid)
    loss = lookup(flags, loss_table)[None]
    feed = lookup(flags, feed_table)[None]
    return heat_mid + flux + heat_release * reaction - loss * heat_mid + feed

def solid_source(temp_pad, temp, heat_new, exchange):
    beside = temp_pad[:, 2:, 1:-1] + temp_pad[:, :-2, 1:-1] + temp_pad[:, 1:-1, 2:] + temp_pad[:, 1:-1, :-2]
    return temp + lateral * (beside - 4.0 * temp) + exchange[None] * (heat_new - temp)

def reduced_matrix(scalars):
    count = scalars.shape[0]
    size = 2 * count
    index = jnp.arange(size)
    segment = index // 2
    odd = index % 2
    rows = scalars[segment]
    first = jnp.where(odd == 0, rows[:, 0], rows[:, 1]) * rows[:, 4]
    last = jnp.where(odd == 0, rows[:, 2], rows[:, 3]) * rows[:, 5]
    cols = index[None, :]
    lower_col = (2 * segment - 1)[:, None]
    upper_col = (2 * segment + 2)[:, None]
    matrix = jnp.eye(size, dtype=scalars.dtype)
    matrix = matrix - jnp.where(cols == lower_col, first[:, None], 0.0)
    matrix = matrix - jnp.where(cols == upper_col, last[:, None], 0.0)
    return matrix

def reference(gas_state, solids_temp, exchange_rate, column_flags, block_inverse, line_coupling):
    reaction = rate_const * gas_state[0] * gas_state[1]
    species_list = []
    for spec in range(NSP):
        padded = jnp.pad(gas_state[spec], 1)[None]
        species_list.append(advance_species(padded, diffusion[spec], stoich[spec], reaction)[0])
    species_new = jnp.stack(species_list)
    mix = 0.5 * jnp.sum(species_new, axis=0)
    heat_new = advance_enthalpy(jnp.pad(gas_state[NSP], 1), jnp.pad(mix, 1), reaction, column_flags)
    gas_next = jnp.concatenate([species_new, heat_new[None]], axis=0)
    temp_pad = jnp.pad(solids_temp, ((0, 0), (1, 1), (1, 1)))
    source = solid_source(temp_pad, solids_temp, heat_new, exchange_rate)
    blocks = block_inverse.reshape(N_SEG, CZ, CZ)
    rhs = source.reshape(N_SEG, CZ, NX * NY)
    local = jnp.einsum('sij,sjc->sic', blocks, rhs, precision=lax.Precision.HIGHEST)
    scalars = jnp.stack([blocks[:, 0, 0], blocks[:, CZ - 1, 0], blocks[:, 0, CZ - 1], blocks[:, CZ - 1, CZ - 1], line_coupling[:, 0], line_coupling[:, 1]], axis=1)
    matrix = reduced_matrix(scalars)
    ends = jnp.stack([local[:, 0], local[:, CZ - 1]], axis=1).reshape(2 * N_SEG, NX * NY)
    interface = jnp.linalg.solve(matrix, ends)
    zero_row = jnp.zeros((1, NX * NY), interface.dtype)
    lasts = interface[1::2]
    firsts = interface[0::2]
    prev_last = jnp.concatenate([zero_row, lasts[:-1]], axis=0)
    next_first = jnp.concatenate([firsts[1:], zero_row], axis=0)
    solved = local + line_coupling[:, 0][:, None, None] * prev_last[:, None, :] * blocks[:, :, 0][:, :, None]
    solved = solved + line_coupling[:, 1][:, None, None] * next_first[:, None, :] * blocks[:, :, CZ - 1][:, :, None]
    return (gas_next, solved.reshape(NZ, NX, NY))
```

```python
import jax
import jax.numpy as jnp
from jax import lax
from jax.experimental import pallas as pl
from jax.experimental.pallas import tpu as pltpu
from jax.sharding import PartitionSpec as P

diffusion = (0.1, 0.08, 0.12, 0.09, 0.11, 0.07)
stoich = (-1.0, -0.5, 1.0, 0.5, 0.25, 0.75)
rate_const = 0.3
upwind = 0.25
cond_base = 0.04
cond_slope = 0.3
heat_release = 0.5
lateral = 0.1
loss_table = (0.0, 0.3, 0.0, 0.1)
feed_table = (0.0, 0.0, 0.4, 0.0)
highest = lax.Precision.HIGHEST


MESH = pl.DeviceIdType.MESH
VMEM = pl.BlockSpec(memory_space=pltpu.VMEM)
ANY = pl.BlockSpec(memory_space=pl.ANY)
F32 = jnp.float32
CHUNK = 16


def shape(*dims):
    return jax.ShapeDtypeStruct(dims, F32)


def params():
    return pltpu.CompilerParams(vmem_limit_bytes=48 * 1024 * 1024)


def iotas(rows, lanes):
    row = lax.broadcasted_iota(jnp.int32, (rows, lanes), 0)
    lane = lax.broadcasted_iota(jnp.int32, (rows, lanes), 1)
    return row, lane


def pack_columns(packed, plane, z, lane, last):
    lanes = plane.shape[1]
    moved = pltpu.roll(plane, lax.rem(z + 1, lanes) if last else z, 1)
    return jnp.where(lane == z, moved, packed)


def shifted(plane, row, lane, z, xlo, xhi, ylo, yhi):
    rows, lanes = plane.shape
    west = jnp.where(row == 0, xlo, pltpu.roll(plane, 1, 0))
    east = jnp.where(row == rows - 1, xhi, pltpu.roll(plane, rows - 1, 0))
    low_col = pltpu.roll(ylo, lax.rem(lanes - z, lanes), 1)
    high_col = pltpu.roll(yhi, lanes - 1 - z, 1)
    south = jnp.where(lane == 0, low_col, pltpu.roll(plane, 1, 1))
    north = jnp.where(lane == lanes - 1, high_col, pltpu.roll(plane, lanes - 1, 1))
    return west, east, south, north


def pack_kernel(gas, temp, x_first, x_last, y_first, y_last):
    step = pl.program_id(0)
    fields = gas.shape[0] + 1
    rows, lanes = gas.shape[2:]
    _, lane = iotas(rows, lanes)

    @pl.when(step == 0)
    def _():
        y_first[...] = jnp.zeros_like(y_first)
        y_last[...] = jnp.zeros_like(y_last)

    for field in range(fields):
        first, last = y_first[field], y_last[field]
        for k in range(gas.shape[1]):
            z = step * gas.shape[1] + k
            plane = gas[field, k] if field < fields - 1 else temp[k]
            first = pack_columns(first, plane, z, lane, False)
            last = pack_columns(last, plane, z, lane, True)
            x_first[field, k : k + 1] = plane[0:1]
            x_last[field, k : k + 1] = plane[rows - 1 : rows]
        y_first[field] = first
        y_last[field] = last


def swap_faces(axes, send_sem, recv_sem):
    barrier = pltpu.get_barrier_semaphore()
    places = []
    for name, *_ in axes:
        here, count = lax.axis_index(name), lax.axis_size(name)
        places.append((here, here > 0, here < count - 1))
    for (name, *_), (here, down, up) in zip(axes, places):
        for exists, step in ((down, -1), (up, 1)):

            @pl.when(exists)
            def _(name=name, here=here, step=step):
                pl.semaphore_signal(barrier, inc=1, device_id={name: here + step}, device_id_type=MESH)

    peers = sum(exists.astype(jnp.int32) for _, *both in places for exists in both)
    pl.semaphore_wait(barrier, peers)

    plan = []
    for index, ((name, first, last, low, high), (here, down, up)) in enumerate(zip(axes, places)):
        to_up = pltpu.make_async_remote_copy(
            src_ref=last, dst_ref=low, send_sem=send_sem.at[2 * index], recv_sem=recv_sem.at[2 * index],
            device_id={name: here + 1}, device_id_type=MESH)
        to_down = pltpu.make_async_remote_copy(
            src_ref=first, dst_ref=high, send_sem=send_sem.at[2 * index + 1], recv_sem=recv_sem.at[2 * index + 1],
            device_id={name: here - 1}, device_id_type=MESH)
        plan.append((to_up, to_down, down, up, low, high))
    for to_up, to_down, down, up, low, high in plan:
        pl.when(up)(to_up.start)
        pl.when(down)(to_down.start)
    for to_up, to_down, down, up, low, high in plan:

        @pl.when(jnp.logical_not(down))
        def _(low=low):
            low[...] = jnp.zeros(low.shape, F32)

        @pl.when(jnp.logical_not(up))
        def _(high=high):
            high[...] = jnp.zeros(high.shape, F32)

    for to_up, to_down, down, up, low, high in plan:
        pl.when(up)(to_up.wait_send)
        pl.when(down)(to_down.wait_send)
        pl.when(down)(to_up.wait_recv)
        pl.when(up)(to_down.wait_recv)


def swap_gas_kernel(z_first, z_last, x_first, x_last, y_first, y_last, zlo, zhi, xlo, xhi, ylo, yhi, send_sem, recv_sem):
    swap_faces(
        (
            ("gx", x_first, x_last, xlo, xhi),
            ("seg", z_first, z_last, zlo, zhi),
            ("gy", y_first, y_last, ylo, yhi),
        ),
        send_sem,
        recv_sem,
    )


def swap(z_first, z_last, x_first, x_last, y_first, y_last, ident):
    faces = (z_first, z_last, x_first, x_last, y_first, y_last)
    return pl.pallas_call(
        swap_gas_kernel,
        out_shape=[shape(*face.shape) for face in faces],
        in_specs=[VMEM] * 6,
        out_specs=[VMEM] * 6,
        scratch_shapes=[pltpu.SemaphoreType.DMA((6,)), pltpu.SemaphoreType.DMA((6,))],
        compiler_params=pltpu.CompilerParams(collective_id=ident, has_side_effects=True),
    )(*faces)


def species_kernel(
    gas, before, after, zlo, zhi, xlo, xhi, ylo, yhi, new, mix_out, z_first, z_last, x_first, x_last, y_first, y_last
):
    step, steps = pl.program_id(0), pl.num_programs(0)
    count, depth, rows, lanes = gas.shape
    row, lane = iotas(rows, lanes)
    at_bottom, at_top = step == 0, step == steps - 1

    @pl.when(step == 0)
    def _():
        y_first[...] = jnp.zeros_like(y_first)
        y_last[...] = jnp.zeros_like(y_last)

    first, last = y_first[...], y_last[...]
    for k in range(depth):
        z = step * depth + k
        reaction = rate_const * gas[0, k] * gas[1, k]
        total = None
        for s in range(count):
            center = gas[s, k]
            below = gas[s, k - 1] if k > 0 else jnp.where(at_bottom, zlo[s], before[s, 0])
            above = gas[s, k + 1] if k < depth - 1 else jnp.where(at_top, zhi[s], after[s, 0])
            west, east, south, north = shifted(
                center, row, lane, z, xlo[s, k : k + 1], xhi[s, k : k + 1], ylo[s], yhi[s]
            )
            beside = (below + above) + (west + east) + (south + north)
            value = (
                center
                + diffusion[s] * (beside - 6.0 * center)
                - upwind * (center - below)
                + stoich[s] * reaction
            )
            new[s, k] = value
            total = value if total is None else total + value
        mix = 0.5 * total
        mix_out[k] = mix
        first = pack_columns(first, mix, z, lane, False)
        last = pack_columns(last, mix, z, lane, True)
        x_first[k : k + 1] = mix[0:1]
        x_last[k : k + 1] = mix[rows - 1 : rows]
        if k == 0:

            @pl.when(at_bottom)
            def _(mix=mix):
                z_first[...] = mix

        if k == depth - 1:

            @pl.when(at_top)
            def _(mix=mix):
                z_last[...] = mix

    y_first[...] = first
    y_last[...] = last


def lookup(flags, table):
    result = jnp.zeros(flags.shape, F32)
    for value, entry in enumerate(table):
        result = result + jnp.where(flags == value, entry, 0.0)
    return result


def energy_kernel(
    pair, heat, heat_before, heat_after, mix, mix_before, mix_after, temp, exchange, flags, inverse, coupling,
    zlo, zhi, xlo, xhi, ylo, yhi, mzlo, mzhi, mxlo, mxhi, mylo, myhi, gas_in,
    heat_out, local, ends, source,
):
    step, steps = pl.program_id(0), pl.num_programs(0)
    depth, rows, lanes = temp.shape
    row, lane = iotas(rows, lanes)
    at_bottom, at_top = step == 0, step == steps - 1
    loss = lookup(flags[...], loss_table)
    feed = lookup(flags[...], feed_table)
    rate = exchange[...]
    for k in range(depth):
        z = step * depth + k
        reaction = rate_const * pair[0, k] * pair[1, k]
        heat_mid, mix_mid, temp_mid = heat[0, k], mix[k], temp[k]
        heat_below = heat[0, k - 1] if k > 0 else jnp.where(at_bottom, zlo[6], heat_before[0, 0])
        heat_above = heat[0, k + 1] if k < depth - 1 else jnp.where(at_top, zhi[6], heat_after[0, 0])
        mix_below = mix[k - 1] if k > 0 else jnp.where(at_bottom, mzlo[...], mix_before[0])
        mix_above = mix[k + 1] if k < depth - 1 else jnp.where(at_top, mzhi[...], mix_after[0])
        one = slice(k, k + 1)
        heats = (heat_below, heat_above) + shifted(
            heat_mid, row, lane, z, xlo[6, one], xhi[6, one], ylo[6], yhi[6]
        )
        mixes = (mix_below, mix_above) + shifted(
            mix_mid, row, lane, z, mxlo[one], mxhi[one], mylo[...], myhi[...]
        )
        temps = shifted(temp_mid, row, lane, z, xlo[7, one], xhi[7, one], ylo[7], yhi[7])
        cond_mid = cond_base + cond_slope * mix_mid
        flux = None
        for heat_near, mix_near in zip(heats, mixes):
            part = (cond_mid + (cond_base + cond_slope * mix_near)) * (heat_near - heat_mid)
            flux = part if flux is None else flux + part
        heat_new = heat_mid + 0.5 * flux + heat_release * reaction - loss * heat_mid + feed
        heat_out[0, k] = heat_new
        beside = (temps[0] + temps[1]) + (temps[2] + temps[3])
        planes = temp_mid + lateral * (beside - 4.0 * temp_mid) + rate * (heat_new - temp_mid)
        source[pl.ds(pl.multiple_of(z * rows, rows), rows), :] = planes

    @pl.when(at_top)
    def _():
        size = inverse.shape[0]
        group = 4
        for start in range(0, rows, group):
            right = jnp.concatenate(
                [source[pl.ds(start + j, size, stride=rows), :] for j in range(group)], axis=1
            )
            result = jnp.dot(inverse[...], right, precision=highest, preferred_element_type=F32)
            for j in range(group):
                local[pl.ds(start + j, size, stride=rows), :] = result[:, j * lanes : (j + 1) * lanes]
        ends[0:rows] = local[0:rows]
        ends[rows : 2 * rows] = local[(size - 1) * rows : size * rows]
        scalars = (
            inverse[0:1, 0:1],
            inverse[size - 1 : size, 0:1],
            inverse[0:1, size - 1 : size],
            inverse[size - 1 : size, size - 1 : size],
            coupling[0:1, 0:1],
            coupling[0:1, 1:2],
        )
        for index, scalar in enumerate(scalars):
            ends[2 * rows + index : 2 * rows + index + 1] = jnp.broadcast_to(scalar, (1, lanes))
        ends[2 * rows + 6 : 2 * rows + 8] = jnp.zeros((2, lanes), F32)


def share_kernel(ends, slots, send_sem, recv_sem):
    here, count = lax.axis_index("seg"), lax.axis_size("seg")
    barrier = pltpu.get_barrier_semaphore()
    for step in range(1, count):
        pl.semaphore_signal(
            barrier, inc=1, device_id={"seg": lax.rem(here + step, count)}, device_id_type=MESH)
    pl.semaphore_wait(barrier, count - 1)
    copies = [
        pltpu.make_async_remote_copy(
            src_ref=ends, dst_ref=slots.at[step], send_sem=send_sem.at[step], recv_sem=recv_sem.at[step],
            device_id={"seg": lax.rem(here + step, count)}, device_id_type=MESH)
        for step in range(1, count)
    ]
    for copy in copies:
        copy.start()
    slots[0] = ends[...]
    for copy in copies:
        copy.wait()


def finish_kernel(slots, local, inverse, out):
    count, total_rows, lanes = slots.shape
    rows = (total_rows - 8) // 2
    size = inverse.shape[0]
    here = lax.axis_index("seg")
    held = [slots[lax.rem(here - s + count, count)] for s in range(count)]
    p_lines, q_lines = [], []
    for s in range(count):
        y_first, y_last = held[s][0:rows], held[s][rows : 2 * rows]
        b00, b90, b09, b99, lower, upper = (held[s][2 * rows + j : 2 * rows + j + 1] for j in range(6))
        p_gain = upper * b09 if s < count - 1 else jnp.zeros_like(upper)
        q_gain = upper * b99 if s < count - 1 else jnp.zeros_like(upper)
        p_const, q_const = y_first, y_last
        if s > 0:
            before_const, before_gain = q_lines[-1]
            into_p, into_q = lower * b00, lower * b90
            scale = 1.0 / (1.0 - into_p * before_gain)
            p_const = (y_first + into_p * before_const) * scale
            p_gain = p_gain * scale
            link = into_q * before_gain
            q_const = y_last + into_q * before_const + link * p_const
            q_gain = q_gain + link * p_gain
        p_lines.append((p_const, p_gain))
        q_lines.append((q_const, q_gain))
    firsts, lasts = [None] * count, [None] * count
    above = jnp.zeros((rows, lanes), F32)
    for s in reversed(range(count)):
        firsts[s] = p_lines[s][0] + p_lines[s][1] * above
        lasts[s] = q_lines[s][0] + q_lines[s][1] * above
        above = firsts[s]
    q_near = jnp.zeros((rows, lanes), F32)
    p_near = jnp.zeros((rows, lanes), F32)
    for s in range(count):
        if s > 0:
            q_near = jnp.where(here == s, lasts[s - 1], q_near)
        if s < count - 1:
            p_near = jnp.where(here == s, firsts[s + 1], p_near)
    mine = slots[0]
    q_near = mine[2 * rows + 4 : 2 * rows + 5] * q_near
    p_near = mine[2 * rows + 5 : 2 * rows + 6] * p_near
    for z in range(size):
        low = jnp.broadcast_to(inverse[z : z + 1, 0:1], (1, lanes))
        high = jnp.broadcast_to(inverse[z : z + 1, size - 1 : size], (1, lanes))
        block = slice(z * rows, (z + 1) * rows)
        out[block] = local[block] + q_near * low + p_near * high


def body(gas_state, solids_temp, exchange_rate, column_flags, block_inverse, line_coupling):
    count = gas_state.shape[0] - 1
    depth, rows, lanes = solids_temp.shape
    segments = lax.axis_size("seg")
    steps = depth // CHUNK
    fields = count + 2

    def fixed(*dims):
        return pl.BlockSpec(dims, lambda i: (0,) * len(dims))

    def stack(number, start):
        return pl.BlockSpec((number, CHUNK, rows, lanes), lambda i: (start, i, 0, 0))

    def below_of(number, start):
        return pl.BlockSpec(
            (number, 1, rows, lanes), lambda i: (start, jnp.maximum(i * CHUNK - 1, 0), 0, 0))

    def above_of(number, start):
        return pl.BlockSpec(
            (number, 1, rows, lanes), lambda i: (start, jnp.minimum((i + 1) * CHUNK, depth - 1), 0, 0))

    planes = pl.BlockSpec((CHUNK, rows, lanes), lambda i: (i, 0, 0))
    edge = pl.BlockSpec((CHUNK, lanes), lambda i: (i, 0))
    edges = pl.BlockSpec((fields, CHUNK, lanes), lambda i: (0, i, 0))
    sides = fixed(fields, rows, lanes)
    tops = fixed(count + 1, rows, lanes)
    side = fixed(rows, lanes)

    x_first, x_last, y_first, y_last = pl.pallas_call(
        pack_kernel,
        grid=(steps,),
        out_shape=[shape(fields, depth, lanes)] * 2 + [shape(fields, rows, lanes)] * 2,
        in_specs=[stack(count + 1, 0), planes],
        out_specs=[edges, edges, sides, sides],
        compiler_params=params(),
    )(gas_state, solids_temp)
    zlo, zhi, xlo, xhi, ylo, yhi = swap(
        gas_state[:, 0], gas_state[:, depth - 1], x_first, x_last, y_first, y_last, 0
    )
    gas_next, mix, mz_first, mz_last, mx_first, mx_last, my_first, my_last = pl.pallas_call(
        species_kernel,
        grid=(steps,),
        out_shape=[shape(count + 1, depth, rows, lanes), shape(depth, rows, lanes)]
        + [shape(rows, lanes)] * 2
        + [shape(depth, lanes)] * 2
        + [shape(rows, lanes)] * 2,
        in_specs=[stack(count, 0), below_of(count, 0), above_of(count, 0), tops, tops, edges, edges, sides, sides],
        out_specs=[stack(count, 0), planes, side, side, edge, edge, side, side],
        compiler_params=params(),
    )(gas_state, gas_state, gas_state, zlo, zhi, xlo, xhi, ylo, yhi)
    mix_halos = swap(mz_first, mz_last, mx_first, mx_last, my_first, my_last, 1)
    mix_below = pl.BlockSpec((1, rows, lanes), lambda i: (jnp.maximum(i * CHUNK - 1, 0), 0, 0))
    mix_above = pl.BlockSpec((1, rows, lanes), lambda i: (jnp.minimum((i + 1) * CHUNK, depth - 1), 0, 0))
    gas_next, local, ends = pl.pallas_call(
        energy_kernel,
        grid=(steps,),
        out_shape=[
            shape(count + 1, depth, rows, lanes),
            shape(depth * rows, lanes),
            shape(2 * rows + 8, lanes),
        ],
        in_specs=[
            stack(2, 0), stack(1, count), below_of(1, count), above_of(1, count),
            planes, mix_below, mix_above, planes, side, side,
            fixed(*block_inverse.shape), fixed(*line_coupling.shape),
            tops, tops, edges, edges, sides, sides,
            side, side, edge, edge, side, side, ANY,
        ],
        out_specs=[stack(1, count), fixed(depth * rows, lanes), fixed(2 * rows + 8, lanes)],
        scratch_shapes=[pltpu.VMEM((depth * rows, lanes), F32)],
        input_output_aliases={24: 0},
        compiler_params=params(),
    )(
        gas_state, gas_state, gas_state, gas_state, mix, mix, mix, solids_temp, exchange_rate, column_flags,
        block_inverse, line_coupling, zlo, zhi, xlo, xhi, ylo, yhi, *mix_halos, gas_next,
    )
    slots = pl.pallas_call(
        share_kernel,
        out_shape=shape(segments, 2 * rows + 8, lanes),
        in_specs=[VMEM],
        out_specs=VMEM,
        scratch_shapes=[pltpu.SemaphoreType.DMA((segments,)), pltpu.SemaphoreType.DMA((segments,))],
        compiler_params=pltpu.CompilerParams(collective_id=2, has_side_effects=True),
    )(ends)
    solved = pl.pallas_call(
        finish_kernel,
        out_shape=shape(depth * rows, lanes),
        in_specs=[VMEM] * 3,
        out_specs=VMEM,
        compiler_params=params(),
    )(slots, local, block_inverse)
    return (gas_next, solved.reshape(depth, rows, lanes))


def solution(mesh):
    in_specs = (
        P(None, "seg", "gx", "gy"),
        P("seg", "gx", "gy"),
        P("gx", "gy"),
        P("gx", "gy"),
        P("seg", None),
        P("seg", None),
    )
    out_specs = (P(None, "seg", "gx", "gy"), P("seg", "gx", "gy"))
    return jax.shard_map(body, mesh=mesh, in_specs=in_specs, out_specs=out_specs, check_vma=False)
```

```python
import jax
import jax.numpy as jnp
from jax import lax
from jax.experimental import pallas as pl
from jax.experimental.pallas import tpu as pltpu
from jax.sharding import PartitionSpec as P

diffusion = (0.1, 0.08, 0.12, 0.09, 0.11, 0.07)
stoich = (-1.0, -0.5, 1.0, 0.5, 0.25, 0.75)
rate_const = 0.3
upwind = 0.25
cond_base = 0.04
cond_slope = 0.3
heat_release = 0.5
lateral = 0.1
loss_table = (0.0, 0.3, 0.0, 0.1)
feed_table = (0.0, 0.0, 0.4, 0.0)
highest = lax.Precision.HIGHEST


MESH = pl.DeviceIdType.MESH
ANY = pl.BlockSpec(memory_space=pl.ANY)
F32 = jnp.float32
CHUNK = 16


def shape(*dims):
    return jax.ShapeDtypeStruct(dims, F32)


def params():
    return pltpu.CompilerParams(vmem_limit_bytes=63 * 1024 * 1024)


def iotas(rows, lanes):
    row = lax.broadcasted_iota(jnp.int32, (rows, lanes), 0)
    lane = lax.broadcasted_iota(jnp.int32, (rows, lanes), 1)
    return row, lane


def pack_columns(packed, plane, z, lane, last):
    lanes = plane.shape[1]
    moved = pltpu.roll(plane, lax.rem(z + 1, lanes) if last else z, 1)
    return jnp.where(lane == z, moved, packed)


def shifted(plane, row, lane, z, xlo, xhi, ylo, yhi):
    rows, lanes = plane.shape
    west = jnp.where(row == 0, xlo, pltpu.roll(plane, 1, 0))
    east = jnp.where(row == rows - 1, xhi, pltpu.roll(plane, rows - 1, 0))
    low_col = pltpu.roll(ylo, lax.rem(lanes - z, lanes), 1)
    high_col = pltpu.roll(yhi, lanes - 1 - z, 1)
    south = jnp.where(lane == 0, low_col, pltpu.roll(plane, 1, 1))
    north = jnp.where(lane == lanes - 1, high_col, pltpu.roll(plane, lanes - 1, 1))
    return west, east, south, north


def pack_kernel(gas, temp, x_first, x_last, y_first, y_last):
    step = pl.program_id(0)
    fields = gas.shape[0] + 1
    rows, lanes = gas.shape[2:]
    _, lane = iotas(rows, lanes)

    @pl.when(step == 0)
    def _():
        y_first[...] = jnp.zeros_like(y_first)
        y_last[...] = jnp.zeros_like(y_last)

    for field in range(fields):
        first, last = y_first[field], y_last[field]
        for k in range(gas.shape[1]):
            z = step * gas.shape[1] + k
            plane = gas[field, k] if field < fields - 1 else temp[k]
            first = pack_columns(first, plane, z, lane, False)
            last = pack_columns(last, plane, z, lane, True)
            x_first[field, k : k + 1] = plane[0:1]
            x_last[field, k : k + 1] = plane[rows - 1 : rows]
        y_first[field] = first
        y_last[field] = last


def swap_faces(axes, blank, zero_sem, send_sem, recv_sem):
    barrier = pltpu.get_barrier_semaphore()
    places = []
    for name, *_ in axes:
        here, count = lax.axis_index(name), lax.axis_size(name)
        places.append((here, here > 0, here < count - 1))
    for (name, *_), (here, down, up) in zip(axes, places):
        for exists, step in ((down, -1), (up, 1)):

            @pl.when(exists)
            def _(name=name, here=here, step=step):
                pl.semaphore_signal(barrier, inc=1, device_id={name: here + step}, device_id_type=MESH)

    peers = sum(exists.astype(jnp.int32) for _, *both in places for exists in both)
    pl.semaphore_wait(barrier, peers)

    plan = []
    for index, ((name, first, last, low, high), (here, down, up)) in enumerate(zip(axes, places)):
        to_up = pltpu.make_async_remote_copy(
            src_ref=last, dst_ref=low, send_sem=send_sem.at[2 * index], recv_sem=recv_sem.at[2 * index],
            device_id={name: here + 1}, device_id_type=MESH)
        to_down = pltpu.make_async_remote_copy(
            src_ref=first, dst_ref=high, send_sem=send_sem.at[2 * index + 1], recv_sem=recv_sem.at[2 * index + 1],
            device_id={name: here - 1}, device_id_type=MESH)
        plan.append((to_up, to_down, down, up, low, high))
    for to_up, to_down, down, up, low, high in plan:
        pl.when(up)(to_up.start)
        pl.when(down)(to_down.start)
    blank[...] = jnp.zeros(blank.shape, F32)
    fills = []
    for index, (_, _, down, up, low, high) in enumerate(plan):
        for side, (exists, halo) in enumerate(((down, low), (up, high))):
            part = blank
            if len(halo.shape) == 2:
                part = blank.at[0, pl.ds(0, halo.shape[0])]
            else:
                part = blank.at[pl.ds(0, halo.shape[0]), pl.ds(0, halo.shape[1])]
            fill = pltpu.make_async_copy(part, halo, zero_sem.at[2 * index + side])
            fills.append((jnp.logical_not(exists), fill))
    for missing, fill in fills:
        pl.when(missing)(fill.start)
    for to_up, to_down, down, up, low, high in plan:
        pl.when(up)(to_up.wait_send)
        pl.when(down)(to_down.wait_send)
        pl.when(down)(to_up.wait_recv)
        pl.when(up)(to_down.wait_recv)
    for missing, fill in fills:
        pl.when(missing)(fill.wait)


def swap_kernel(
    field, x_first, x_last, y_first, y_last, zlo, zhi, xlo, xhi, ylo, yhi, blank, zero_sem, send_sem, recv_sem
):
    if len(field.shape) == 4:
        z_first, z_last = field.at[:, 0], field.at[:, field.shape[1] - 1]
    else:
        z_first, z_last = field.at[0], field.at[field.shape[0] - 1]
    swap_faces(
        (
            ("gx", x_first, x_last, xlo, xhi),
            ("seg", z_first, z_last, zlo, zhi),
            ("gy", y_first, y_last, ylo, yhi),
        ),
        blank,
        zero_sem,
        send_sem,
        recv_sem,
    )


def swap(field, x_first, x_last, y_first, y_last, ident):
    top = shape(*field.shape[:-3], *field.shape[-2:])
    side = shape(*x_first.shape)
    edge = shape(*y_first.shape)
    blank = (1,) * (3 - x_first.ndim) + x_first.shape
    sems = pltpu.SemaphoreType.DMA((6,))
    return pl.pallas_call(
        swap_kernel,
        out_shape=[top, top, side, side, edge, edge],
        in_specs=[ANY] * 5,
        out_specs=[ANY] * 6,
        scratch_shapes=[pltpu.VMEM(blank, F32), sems, sems, sems],
        compiler_params=pltpu.CompilerParams(collective_id=ident, has_side_effects=True, vmem_limit_bytes=63 * 1024 * 1024),
    )(field, x_first, x_last, y_first, y_last)


def species_kernel(
    gas, before, after, zlo, zhi, xlo, xhi, ylo, yhi, new, mix_out, x_first, x_last, y_first, y_last
):
    step, steps = pl.program_id(0), pl.num_programs(0)
    count, depth, rows, lanes = gas.shape
    row, lane = iotas(rows, lanes)
    at_bottom, at_top = step == 0, step == steps - 1

    @pl.when(step == 0)
    def _():
        y_first[...] = jnp.zeros_like(y_first)
        y_last[...] = jnp.zeros_like(y_last)

    first, last = y_first[...], y_last[...]
    for k in range(depth):
        z = step * depth + k
        reaction = rate_const * gas[0, k] * gas[1, k]
        total = None
        for s in range(count):
            center = gas[s, k]
            below = gas[s, k - 1] if k > 0 else jnp.where(at_bottom, zlo[s], before[s, 0])
            above = gas[s, k + 1] if k < depth - 1 else jnp.where(at_top, zhi[s], after[s, 0])
            west, east, south, north = shifted(
                center, row, lane, z, xlo[s, k : k + 1], xhi[s, k : k + 1], ylo[s], yhi[s]
            )
            beside = (below + above) + (west + east) + (south + north)
            value = (
                center
                + diffusion[s] * (beside - 6.0 * center)
                - upwind * (center - below)
                + stoich[s] * reaction
            )
            new[s, k] = value
            total = value if total is None else total + value
        mix = 0.5 * total
        mix_out[k] = mix
        first = pack_columns(first, mix, z, lane, False)
        last = pack_columns(last, mix, z, lane, True)
        x_first[k : k + 1] = mix[0:1]
        x_last[k : k + 1] = mix[rows - 1 : rows]
    y_first[...] = first
    y_last[...] = last


def lookup(flags, table):
    result = jnp.zeros(flags.shape, F32)
    for value, entry in enumerate(table):
        result = result + jnp.where(flags == value, entry, 0.0)
    return result


def energy_kernel(
    pair, heat, heat_before, heat_after, mix, mix_before, mix_after, temp, exchange, flags, inverse, coupling,
    zlo, zhi, xlo, xhi, ylo, yhi, mzlo, mzhi, mxlo, mxhi, mylo, myhi, gas_in,
    heat_out, local, ends, source,
):
    step, steps = pl.program_id(0), pl.num_programs(0)
    depth, rows, lanes = temp.shape
    row, lane = iotas(rows, lanes)
    at_bottom, at_top = step == 0, step == steps - 1
    loss = lookup(flags[...], loss_table)
    feed = lookup(flags[...], feed_table)
    rate = exchange[...]
    for k in range(depth):
        z = step * depth + k
        reaction = rate_const * pair[0, k] * pair[1, k]
        heat_mid, mix_mid, temp_mid = heat[0, k], mix[k], temp[k]
        heat_below = heat[0, k - 1] if k > 0 else jnp.where(at_bottom, zlo[6], heat_before[0, 0])
        heat_above = heat[0, k + 1] if k < depth - 1 else jnp.where(at_top, zhi[6], heat_after[0, 0])
        mix_below = mix[k - 1] if k > 0 else jnp.where(at_bottom, mzlo[...], mix_before[0])
        mix_above = mix[k + 1] if k < depth - 1 else jnp.where(at_top, mzhi[...], mix_after[0])
        one = slice(k, k + 1)
        heats = (heat_below, heat_above) + shifted(
            heat_mid, row, lane, z, xlo[6, one], xhi[6, one], ylo[6], yhi[6]
        )
        mixes = (mix_below, mix_above) + shifted(
            mix_mid, row, lane, z, mxlo[one], mxhi[one], mylo[...], myhi[...]
        )
        temps = shifted(temp_mid, row, lane, z, xlo[7, one], xhi[7, one], ylo[7], yhi[7])
        cond_mid = cond_base + cond_slope * mix_mid
        flux = None
        for heat_near, mix_near in zip(heats, mixes):
            part = (cond_mid + (cond_base + cond_slope * mix_near)) * (heat_near - heat_mid)
            flux = part if flux is None else flux + part
        heat_new = heat_mid + 0.5 * flux + heat_release * reaction - loss * heat_mid + feed
        heat_out[0, k] = heat_new
        beside = (temps[0] + temps[1]) + (temps[2] + temps[3])
        planes = temp_mid + lateral * (beside - 4.0 * temp_mid) + rate * (heat_new - temp_mid)
        source[pl.ds(pl.multiple_of(z * rows, rows), rows), :] = planes

    @pl.when(at_top)
    def _():
        size = inverse.shape[0]
        group = 4
        for start in range(0, rows, group):
            right = jnp.concatenate(
                [source[pl.ds(start + j, size, stride=rows), :] for j in range(group)], axis=1
            )
            result = jnp.dot(inverse[...], right, precision=highest, preferred_element_type=F32)
            for j in range(group):
                local[pl.ds(start + j, size, stride=rows), :] = result[:, j * lanes : (j + 1) * lanes]
        ends[0:rows] = local[0:rows]
        ends[rows : 2 * rows] = local[(size - 1) * rows : size * rows]
        scalars = (
            inverse[0:1, 0:1],
            inverse[size - 1 : size, 0:1],
            inverse[0:1, size - 1 : size],
            inverse[size - 1 : size, size - 1 : size],
            coupling[0:1, 0:1],
            coupling[0:1, 1:2],
        )
        for index, scalar in enumerate(scalars):
            ends[2 * rows + index : 2 * rows + index + 1] = jnp.broadcast_to(scalar, (1, lanes))
        ends[2 * rows + 6 : 2 * rows + 8] = jnp.zeros((2, lanes), F32)


def share_kernel(ends, slots, own_sem, send_sem, recv_sem):
    here, count = lax.axis_index("seg"), lax.axis_size("seg")
    barrier = pltpu.get_barrier_semaphore()
    for step in range(1, count):
        pl.semaphore_signal(
            barrier, inc=1, device_id={"seg": lax.rem(here + step, count)}, device_id_type=MESH)
    pl.semaphore_wait(barrier, count - 1)
    copies = [
        pltpu.make_async_remote_copy(
            src_ref=ends, dst_ref=slots.at[step], send_sem=send_sem.at[step], recv_sem=recv_sem.at[step],
            device_id={"seg": lax.rem(here + step, count)}, device_id_type=MESH)
        for step in range(1, count)
    ]
    for copy in copies:
        copy.start()
    own = pltpu.make_async_copy(ends, slots.at[0], own_sem)
    own.start()
    own.wait()
    for copy in copies:
        copy.wait()


def finish_kernel(slots, local, inverse, out):
    count, total_rows, lanes = slots.shape
    rows = (total_rows - 8) // 2
    size, width = inverse.shape
    here = lax.axis_index("seg")
    held = [slots[lax.rem(here - s + count, count)] for s in range(count)]
    p_lines, q_lines = [], []
    for s in range(count):
        y_first, y_last = held[s][0:rows], held[s][rows : 2 * rows]
        b00, b90, b09, b99, lower, upper = (held[s][2 * rows + j : 2 * rows + j + 1] for j in range(6))
        p_gain = upper * b09 if s < count - 1 else jnp.zeros_like(upper)
        q_gain = upper * b99 if s < count - 1 else jnp.zeros_like(upper)
        p_const, q_const = y_first, y_last
        if s > 0:
            before_const, before_gain = q_lines[-1]
            into_p, into_q = lower * b00, lower * b90
            scale = 1.0 / (1.0 - into_p * before_gain)
            p_const = (y_first + into_p * before_const) * scale
            p_gain = p_gain * scale
            link = into_q * before_gain
            q_const = y_last + into_q * before_const + link * p_const
            q_gain = q_gain + link * p_gain
        p_lines.append((p_const, p_gain))
        q_lines.append((q_const, q_gain))
    firsts, lasts = [None] * count, [None] * count
    above = jnp.zeros((rows, lanes), F32)
    for s in reversed(range(count)):
        firsts[s] = p_lines[s][0] + p_lines[s][1] * above
        lasts[s] = q_lines[s][0] + q_lines[s][1] * above
        above = firsts[s]
    q_near = jnp.zeros((rows, lanes), F32)
    p_near = jnp.zeros((rows, lanes), F32)
    for s in range(count):
        if s > 0:
            q_near = jnp.where(here == s, lasts[s - 1], q_near)
        if s < count - 1:
            p_near = jnp.where(here == s, firsts[s + 1], p_near)
    mine = slots[0]
    q_near = mine[2 * rows + 4 : 2 * rows + 5] * q_near
    p_near = mine[2 * rows + 5 : 2 * rows + 6] * p_near
    for z in range(size):
        low = jnp.broadcast_to(inverse[z : z + 1, 0:1], (1, lanes))
        high = jnp.broadcast_to(inverse[z : z + 1, width - 1 : width], (1, lanes))
        block = slice(z * rows, (z + 1) * rows)
        out[block] = local[block] + q_near * low + p_near * high


def body(gas_state, solids_temp, exchange_rate, column_flags, block_inverse, line_coupling):
    count = gas_state.shape[0] - 1
    depth, rows, lanes = solids_temp.shape
    segments = lax.axis_size("seg")
    steps = depth // CHUNK
    fields = count + 2

    def fixed(*dims):
        return pl.BlockSpec(dims, lambda i: (0,) * len(dims))

    def stack(number, start):
        return pl.BlockSpec((number, CHUNK, rows, lanes), lambda i: (start, i, 0, 0))

    def below_of(number, start):
        return pl.BlockSpec(
            (number, 1, rows, lanes), lambda i: (start, jnp.maximum(i * CHUNK - 1, 0), 0, 0))

    def above_of(number, start):
        return pl.BlockSpec(
            (number, 1, rows, lanes), lambda i: (start, jnp.minimum((i + 1) * CHUNK, depth - 1), 0, 0))

    planes = pl.BlockSpec((CHUNK, rows, lanes), lambda i: (i, 0, 0))
    edge = pl.BlockSpec((CHUNK, lanes), lambda i: (i, 0))
    edges = pl.BlockSpec((fields, CHUNK, lanes), lambda i: (0, i, 0))
    sides = fixed(fields, rows, lanes)
    tops = fixed(count + 1, rows, lanes)
    side = fixed(rows, lanes)

    x_first, x_last, y_first, y_last = pl.pallas_call(
        pack_kernel,
        grid=(steps,),
        out_shape=[shape(fields, depth, lanes)] * 2 + [shape(fields, rows, lanes)] * 2,
        in_specs=[stack(count + 1, 0), planes],
        out_specs=[edges, edges, sides, sides],
        compiler_params=params(),
    )(gas_state, solids_temp)
    zlo, zhi, xlo, xhi, ylo, yhi = swap(
        gas_state, x_first, x_last, y_first, y_last, 0
    )
    gas_next, mix, mx_first, mx_last, my_first, my_last = pl.pallas_call(
        species_kernel,
        grid=(steps,),
        out_shape=[shape(count + 1, depth, rows, lanes), shape(depth, rows, lanes)]
        + [shape(depth, lanes)] * 2
        + [shape(rows, lanes)] * 2,
        in_specs=[stack(count, 0), below_of(count, 0), above_of(count, 0), tops, tops, edges, edges, sides, sides],
        out_specs=[stack(count, 0), planes, edge, edge, side, side],
        compiler_params=params(),
    )(gas_state, gas_state, gas_state, zlo, zhi, xlo, xhi, ylo, yhi)
    mix_halos = swap(mix, mx_first, mx_last, my_first, my_last, 1)
    mix_below = pl.BlockSpec((1, rows, lanes), lambda i: (jnp.maximum(i * CHUNK - 1, 0), 0, 0))
    mix_above = pl.BlockSpec((1, rows, lanes), lambda i: (jnp.minimum((i + 1) * CHUNK, depth - 1), 0, 0))
    gas_next, local, ends = pl.pallas_call(
        energy_kernel,
        grid=(steps,),
        out_shape=[
            shape(count + 1, depth, rows, lanes),
            shape(depth * rows, lanes),
            shape(2 * rows + 8, lanes),
        ],
        in_specs=[
            stack(2, 0), stack(1, count), below_of(1, count), above_of(1, count),
            planes, mix_below, mix_above, planes, side, side,
            fixed(*block_inverse.shape), fixed(*line_coupling.shape),
            tops, tops, edges, edges, sides, sides,
            side, side, edge, edge, side, side, ANY,
        ],
        out_specs=[stack(1, count), fixed(depth * rows, lanes), fixed(2 * rows + 8, lanes)],
        scratch_shapes=[pltpu.VMEM((depth * rows, lanes), F32)],
        input_output_aliases={24: 0},
        compiler_params=params(),
    )(
        gas_state, gas_state, gas_state, gas_state, mix, mix, mix, solids_temp, exchange_rate, column_flags,
        block_inverse, line_coupling, zlo, zhi, xlo, xhi, ylo, yhi, *mix_halos, gas_next,
    )
    slots = pl.pallas_call(
        share_kernel,
        out_shape=shape(segments, 2 * rows + 8, lanes),
        in_specs=[ANY],
        out_specs=ANY,
        scratch_shapes=[pltpu.SemaphoreType.DMA(()), pltpu.SemaphoreType.DMA((segments,)), pltpu.SemaphoreType.DMA((segments,))],
        compiler_params=pltpu.CompilerParams(collective_id=2, has_side_effects=True, vmem_limit_bytes=63 * 1024 * 1024),
    )(ends)
    part = 2 * CHUNK
    solved = pl.pallas_call(
        finish_kernel,
        out_shape=shape(depth * rows, lanes),
        grid=(depth // part,),
        in_specs=[
            fixed(segments, 2 * rows + 8, lanes),
            pl.BlockSpec((part * rows, lanes), lambda i: (i, 0)),
            pl.BlockSpec((part, depth), lambda i: (i, 0)),
        ],
        out_specs=pl.BlockSpec((part * rows, lanes), lambda i: (i, 0)),
        compiler_params=params(),
    )(slots, local, block_inverse)
    return (gas_next, solved.reshape(depth, rows, lanes))


def solution(mesh):
    in_specs = (
        P(None, "seg", "gx", "gy"),
        P("seg", "gx", "gy"),
        P("gx", "gy"),
        P("gx", "gy"),
        P("seg", None),
        P("seg", None),
    )
    out_specs = (P(None, "seg", "gx", "gy"), P("seg", "gx", "gy"))
    return jax.shard_map(body, mesh=mesh, in_specs=in_specs, out_specs=out_specs, check_vma=False)
```

```python
import jax
import jax.numpy as jnp
from jax import lax
from jax.experimental import pallas as pl
from jax.experimental.pallas import tpu as pltpu
from jax.sharding import PartitionSpec as P

diffusion = (0.1, 0.08, 0.12, 0.09, 0.11, 0.07)
stoich = (-1.0, -0.5, 1.0, 0.5, 0.25, 0.75)
rate_const = 0.3
upwind = 0.25
cond_base = 0.04
cond_slope = 0.3
heat_release = 0.5
lateral = 0.1
loss_table = (0.0, 0.3, 0.0, 0.1)
feed_table = (0.0, 0.0, 0.4, 0.0)
highest = lax.Precision.HIGHEST


MESH = pl.DeviceIdType.MESH
ANY = pl.BlockSpec(memory_space=pl.ANY)
F32 = jnp.float32
CHUNK = 16


def shape(*dims):
    return jax.ShapeDtypeStruct(dims, F32)


def params():
    return pltpu.CompilerParams(vmem_limit_bytes=63 * 1024 * 1024)


def iotas(rows, lanes):
    row = lax.broadcasted_iota(jnp.int32, (rows, lanes), 0)
    lane = lax.broadcasted_iota(jnp.int32, (rows, lanes), 1)
    return row, lane


def pack_columns(packed, plane, k, lane):
    lanes = plane.shape[1]
    moved = pltpu.roll(plane, 2 * k, 1) if k else plane
    ours = (lane == 2 * k) | (lane == (2 * k - 1) % lanes)
    return jnp.where(ours, moved, packed)


def page_of(step, lanes):
    per_page = lanes // (2 * CHUNK)
    return step // per_page, lax.rem(step, per_page) * (2 * CHUNK)


def merge_pages(low, high, lane):
    lanes = low.shape[1]
    return jnp.where(lane % 2 == 0, pltpu.roll(low, 1, 1), pltpu.roll(high, lanes - 1, 1))


def chunk_halo(low, high, step, lane):
    lanes = low.shape[1]
    _, offset = page_of(step, lanes)
    return pltpu.roll(merge_pages(low, high, lane), lax.rem(lanes - offset, lanes), 1)


def shifted(plane, row, lane, k, xlo, xhi, halo):
    rows, lanes = plane.shape
    west = jnp.where(row == 0, xlo, pltpu.roll(plane, 1, 0))
    east = jnp.where(row == rows - 1, xhi, pltpu.roll(plane, rows - 1, 0))
    column = pltpu.roll(halo, lanes - 2 * k, 1) if k else halo
    south = jnp.where(lane == 0, column, pltpu.roll(plane, 1, 1))
    north = jnp.where(lane == lanes - 1, column, pltpu.roll(plane, lanes - 1, 1))
    return west, east, south, north


def pack_kernel(gas, temp, x_first, x_last, y_pair):
    step = pl.program_id(0)
    fields = gas.shape[0] + 1
    rows, lanes = gas.shape[2:]
    _, lane = iotas(rows, lanes)

    @pl.when(step == 0)
    def _():
        y_pair[...] = jnp.zeros_like(y_pair)

    page, offset = page_of(step, lanes)
    for field in range(fields):
        packed = jnp.zeros((rows, lanes), F32)
        for k in range(gas.shape[1]):
            plane = gas[field, k] if field < fields - 1 else temp[k]
            packed = pack_columns(packed, plane, k, lane)
            x_first[field, k : k + 1] = plane[0:1]
            x_last[field, k : k + 1] = plane[rows - 1 : rows]
        y_pair[page, field] += pltpu.roll(packed, offset, 1)


def swap_faces(axes, blanks, zero_sem, send_sem, recv_sem):
    barrier = pltpu.get_barrier_semaphore()
    places = []
    for name, *_ in axes:
        here, count = lax.axis_index(name), lax.axis_size(name)
        places.append((here, here > 0, here < count - 1))
    for (name, *_), (here, down, up) in zip(axes, places):
        for exists, step in ((down, -1), (up, 1)):

            @pl.when(exists)
            def _(name=name, here=here, step=step):
                pl.semaphore_signal(barrier, inc=1, device_id={name: here + step}, device_id_type=MESH)

    peers = sum(exists.astype(jnp.int32) for _, *both in places for exists in both)
    pl.semaphore_wait(barrier, peers)

    plan = []
    for index, ((name, first, last, low, high), (here, down, up)) in enumerate(zip(axes, places)):
        to_up = pltpu.make_async_remote_copy(
            src_ref=last, dst_ref=low, send_sem=send_sem.at[2 * index], recv_sem=recv_sem.at[2 * index],
            device_id={name: here + 1}, device_id_type=MESH)
        to_down = pltpu.make_async_remote_copy(
            src_ref=first, dst_ref=high, send_sem=send_sem.at[2 * index + 1], recv_sem=recv_sem.at[2 * index + 1],
            device_id={name: here - 1}, device_id_type=MESH)
        plan.append((to_up, to_down, down, up, low, high))
    for to_up, to_down, down, up, low, high in plan:
        pl.when(up)(to_up.start)
        pl.when(down)(to_down.start)
    for blank in blanks:
        blank[...] = jnp.zeros(blank.shape, F32)
    fills = []
    for index, (_, _, down, up, low, high) in enumerate(plan):
        for side, (exists, halo) in enumerate(((down, low), (up, high))):
            fill = pltpu.make_async_copy(blanks[index], halo, zero_sem.at[2 * index + side])
            fills.append((jnp.logical_not(exists), fill))
    for missing, fill in fills:
        pl.when(missing)(fill.start)
    for to_up, to_down, down, up, low, high in plan:
        pl.when(up)(to_up.wait_send)
        pl.when(down)(to_down.wait_send)
        pl.when(down)(to_up.wait_recv)
        pl.when(up)(to_down.wait_recv)
    for missing, fill in fills:
        pl.when(missing)(fill.wait)


def swap_kernel(
    field, x_first, x_last, y_pair, zlo, zhi, xlo, xhi, ylo, yhi, x_blank, z_blank, y_blank, zero_sem, send_sem, recv_sem
):
    if len(field.shape) == 4:
        z_first, z_last = field.at[:, 0], field.at[:, field.shape[1] - 1]
    else:
        z_first, z_last = field.at[0], field.at[field.shape[0] - 1]
    swap_faces(
        (
            ("gx", x_first, x_last, xlo, xhi),
            ("seg", z_first, z_last, zlo, zhi),
            ("gy", y_pair, y_pair, ylo, yhi),
        ),
        (x_blank, z_blank, y_blank),
        zero_sem,
        send_sem,
        recv_sem,
    )


def swap(field, x_first, x_last, y_pair, ident):
    top = shape(*field.shape[:-3], *field.shape[-2:])
    side = shape(*x_first.shape)
    edge = shape(*y_pair.shape)
    sems = pltpu.SemaphoreType.DMA((6,))
    return pl.pallas_call(
        swap_kernel,
        out_shape=[top, top, side, side, edge, edge],
        in_specs=[ANY] * 4,
        out_specs=[ANY] * 6,
        scratch_shapes=[pltpu.VMEM(face.shape, F32) for face in (side, top, edge)] + [sems, sems, sems],
        compiler_params=pltpu.CompilerParams(collective_id=ident, has_side_effects=True, vmem_limit_bytes=63 * 1024 * 1024),
    )(field, x_first, x_last, y_pair)


def species_kernel(
    gas, before, after, zlo, zhi, xlo, xhi, ylo, yhi, new, mix_out, x_first, x_last, y_pair
):
    step, steps = pl.program_id(0), pl.num_programs(0)
    count, depth, rows, lanes = gas.shape
    row, lane = iotas(rows, lanes)
    at_bottom, at_top = step == 0, step == steps - 1

    @pl.when(step == 0)
    def _():
        y_pair[...] = jnp.zeros_like(y_pair)

    page, offset = page_of(step, lanes)
    packed = jnp.zeros((rows, lanes), F32)
    halos = [chunk_halo(ylo[page, s], yhi[page, s], step, lane) for s in range(count)]
    for k in range(depth):
        reaction = rate_const * gas[0, k] * gas[1, k]
        total = None
        for s in range(count):
            center = gas[s, k]
            below = gas[s, k - 1] if k > 0 else jnp.where(at_bottom, zlo[s], before[s, 0])
            above = gas[s, k + 1] if k < depth - 1 else jnp.where(at_top, zhi[s], after[s, 0])
            west, east, south, north = shifted(
                center, row, lane, k, xlo[s, k : k + 1], xhi[s, k : k + 1], halos[s]
            )
            beside = (below + above) + (west + east) + (south + north)
            value = (
                center
                + diffusion[s] * (beside - 6.0 * center)
                - upwind * (center - below)
                + stoich[s] * reaction
            )
            new[s, k] = value
            total = value if total is None else total + value
        mix = 0.5 * total
        mix_out[k] = mix
        packed = pack_columns(packed, mix, k, lane)
        x_first[k : k + 1] = mix[0:1]
        x_last[k : k + 1] = mix[rows - 1 : rows]
    y_pair[page] += pltpu.roll(packed, offset, 1)


def lookup(flags, table):
    result = jnp.zeros(flags.shape, F32)
    for value, entry in enumerate(table):
        result = result + jnp.where(flags == value, entry, 0.0)
    return result


def energy_kernel(
    pair, heat, heat_before, heat_after, mix, mix_before, mix_after, temp, exchange, flags, inverse, coupling,
    zlo, zhi, xlo, xhi, ylo, yhi, mzlo, mzhi, mxlo, mxhi, mylo, myhi, gas_in,
    heat_out, local, ends, source,
):
    step, steps = pl.program_id(0), pl.num_programs(0)
    depth, rows, lanes = temp.shape
    row, lane = iotas(rows, lanes)
    at_bottom, at_top = step == 0, step == steps - 1
    loss = lookup(flags[...], loss_table)
    feed = lookup(flags[...], feed_table)
    rate = exchange[...]
    page, _ = page_of(step, lanes)
    heat_halo = chunk_halo(ylo[page, 6], yhi[page, 6], step, lane)
    temp_halo = chunk_halo(ylo[page, 7], yhi[page, 7], step, lane)
    mix_halo = chunk_halo(mylo[page], myhi[page], step, lane)
    for k in range(depth):
        z = step * depth + k
        reaction = rate_const * pair[0, k] * pair[1, k]
        heat_mid, mix_mid, temp_mid = heat[0, k], mix[k], temp[k]
        heat_below = heat[0, k - 1] if k > 0 else jnp.where(at_bottom, zlo[6], heat_before[0, 0])
        heat_above = heat[0, k + 1] if k < depth - 1 else jnp.where(at_top, zhi[6], heat_after[0, 0])
        mix_below = mix[k - 1] if k > 0 else jnp.where(at_bottom, mzlo[...], mix_before[0])
        mix_above = mix[k + 1] if k < depth - 1 else jnp.where(at_top, mzhi[...], mix_after[0])
        one = slice(k, k + 1)
        heats = (heat_below, heat_above) + shifted(
            heat_mid, row, lane, k, xlo[6, one], xhi[6, one], heat_halo
        )
        mixes = (mix_below, mix_above) + shifted(
            mix_mid, row, lane, k, mxlo[one], mxhi[one], mix_halo
        )
        temps = shifted(temp_mid, row, lane, k, xlo[7, one], xhi[7, one], temp_halo)
        cond_mid = cond_base + cond_slope * mix_mid
        flux = None
        for heat_near, mix_near in zip(heats, mixes):
            part = (cond_mid + (cond_base + cond_slope * mix_near)) * (heat_near - heat_mid)
            flux = part if flux is None else flux + part
        heat_new = heat_mid + 0.5 * flux + heat_release * reaction - loss * heat_mid + feed
        heat_out[0, k] = heat_new
        beside = (temps[0] + temps[1]) + (temps[2] + temps[3])
        planes = temp_mid + lateral * (beside - 4.0 * temp_mid) + rate * (heat_new - temp_mid)
        source[pl.ds(pl.multiple_of(z * rows, rows), rows), :] = planes

    @pl.when(at_top)
    def _():
        size = inverse.shape[0]
        group = 4
        for start in range(0, rows, group):
            right = jnp.concatenate(
                [source[pl.ds(start + j, size, stride=rows), :] for j in range(group)], axis=1
            )
            result = jnp.dot(inverse[...], right, precision=highest, preferred_element_type=F32)
            for j in range(group):
                local[pl.ds(start + j, size, stride=rows), :] = result[:, j * lanes : (j + 1) * lanes]
        ends[0:rows] = local[0:rows]
        ends[rows : 2 * rows] = local[(size - 1) * rows : size * rows]
        scalars = (
            inverse[0:1, 0:1],
            inverse[size - 1 : size, 0:1],
            inverse[0:1, size - 1 : size],
            inverse[size - 1 : size, size - 1 : size],
            coupling[0:1, 0:1],
            coupling[0:1, 1:2],
        )
        for index, scalar in enumerate(scalars):
            ends[2 * rows + index : 2 * rows + index + 1] = jnp.broadcast_to(scalar, (1, lanes))
        ends[2 * rows + 6 : 2 * rows + 8] = jnp.zeros((2, lanes), F32)


def share_kernel(ends, slots, own_sem, send_sem, recv_sem):
    here, count = lax.axis_index("seg"), lax.axis_size("seg")
    barrier = pltpu.get_barrier_semaphore()
    for step in range(1, count):
        pl.semaphore_signal(
            barrier, inc=1, device_id={"seg": lax.rem(here + step, count)}, device_id_type=MESH)
    pl.semaphore_wait(barrier, count - 1)
    copies = [
        pltpu.make_async_remote_copy(
            src_ref=ends, dst_ref=slots.at[step], send_sem=send_sem.at[step], recv_sem=recv_sem.at[step],
            device_id={"seg": lax.rem(here + step, count)}, device_id_type=MESH)
        for step in range(1, count)
    ]
    for copy in copies:
        copy.start()
    own = pltpu.make_async_copy(ends, slots.at[0], own_sem)
    own.start()
    own.wait()
    for copy in copies:
        copy.wait()


def finish_kernel(slots, local, inverse, out):
    count, total_rows, lanes = slots.shape
    rows = (total_rows - 8) // 2
    size, width = inverse.shape
    here = lax.axis_index("seg")
    held = [slots[lax.rem(here - s + count, count)] for s in range(count)]
    p_lines, q_lines = [], []
    for s in range(count):
        y_first, y_last = held[s][0:rows], held[s][rows : 2 * rows]
        b00, b90, b09, b99, lower, upper = (held[s][2 * rows + j : 2 * rows + j + 1] for j in range(6))
        p_gain = upper * b09 if s < count - 1 else jnp.zeros_like(upper)
        q_gain = upper * b99 if s < count - 1 else jnp.zeros_like(upper)
        p_const, q_const = y_first, y_last
        if s > 0:
            before_const, before_gain = q_lines[-1]
            into_p, into_q = lower * b00, lower * b90
            scale = 1.0 / (1.0 - into_p * before_gain)
            p_const = (y_first + into_p * before_const) * scale
            p_gain = p_gain * scale
            link = into_q * before_gain
            q_const = y_last + into_q * before_const + link * p_const
            q_gain = q_gain + link * p_gain
        p_lines.append((p_const, p_gain))
        q_lines.append((q_const, q_gain))
    firsts, lasts = [None] * count, [None] * count
    above = jnp.zeros((rows, lanes), F32)
    for s in reversed(range(count)):
        firsts[s] = p_lines[s][0] + p_lines[s][1] * above
        lasts[s] = q_lines[s][0] + q_lines[s][1] * above
        above = firsts[s]
    q_near = jnp.zeros((rows, lanes), F32)
    p_near = jnp.zeros((rows, lanes), F32)
    for s in range(count):
        if s > 0:
            q_near = jnp.where(here == s, lasts[s - 1], q_near)
        if s < count - 1:
            p_near = jnp.where(here == s, firsts[s + 1], p_near)
    mine = slots[0]
    q_near = mine[2 * rows + 4 : 2 * rows + 5] * q_near
    p_near = mine[2 * rows + 5 : 2 * rows + 6] * p_near
    for z in range(size):
        low = jnp.broadcast_to(inverse[z : z + 1, 0:1], (1, lanes))
        high = jnp.broadcast_to(inverse[z : z + 1, width - 1 : width], (1, lanes))
        block = slice(z * rows, (z + 1) * rows)
        out[block] = local[block] + q_near * low + p_near * high


def body(gas_state, solids_temp, exchange_rate, column_flags, block_inverse, line_coupling):
    count = gas_state.shape[0] - 1
    depth, rows, lanes = solids_temp.shape
    segments = lax.axis_size("seg")
    steps = depth // CHUNK
    fields = count + 2

    def fixed(*dims):
        return pl.BlockSpec(dims, lambda i: (0,) * len(dims))

    def stack(number, start):
        return pl.BlockSpec((number, CHUNK, rows, lanes), lambda i: (start, i, 0, 0))

    def below_of(number, start):
        return pl.BlockSpec(
            (number, 1, rows, lanes), lambda i: (start, jnp.maximum(i * CHUNK - 1, 0), 0, 0))

    def above_of(number, start):
        return pl.BlockSpec(
            (number, 1, rows, lanes), lambda i: (start, jnp.minimum((i + 1) * CHUNK, depth - 1), 0, 0))

    planes = pl.BlockSpec((CHUNK, rows, lanes), lambda i: (i, 0, 0))
    edge = pl.BlockSpec((CHUNK, lanes), lambda i: (i, 0))
    edges = pl.BlockSpec((fields, CHUNK, lanes), lambda i: (0, i, 0))
    pages = -(-2 * depth // lanes)
    sides = fixed(pages, fields, rows, lanes)
    tops = fixed(count + 1, rows, lanes)
    side = fixed(rows, lanes)
    mix_sides = fixed(pages, rows, lanes)

    x_first, x_last, y_pair = pl.pallas_call(
        pack_kernel,
        grid=(steps,),
        out_shape=[shape(fields, depth, lanes)] * 2 + [shape(pages, fields, rows, lanes)],
        in_specs=[stack(count + 1, 0), planes],
        out_specs=[edges, edges, sides],
        compiler_params=params(),
    )(gas_state, solids_temp)
    zlo, zhi, xlo, xhi, ylo, yhi = swap(
        gas_state, x_first, x_last, y_pair, 0
    )
    gas_next, mix, mx_first, mx_last, my_pair = pl.pallas_call(
        species_kernel,
        grid=(steps,),
        out_shape=[shape(count + 1, depth, rows, lanes), shape(depth, rows, lanes)]
        + [shape(depth, lanes)] * 2
        + [shape(pages, rows, lanes)],
        in_specs=[stack(count, 0), below_of(count, 0), above_of(count, 0), tops, tops, edges, edges, sides, sides],
        out_specs=[stack(count, 0), planes, edge, edge, mix_sides],
        compiler_params=params(),
    )(gas_state, gas_state, gas_state, zlo, zhi, xlo, xhi, ylo, yhi)
    mix_halos = swap(mix, mx_first, mx_last, my_pair, 1)
    mix_below = pl.BlockSpec((1, rows, lanes), lambda i: (jnp.maximum(i * CHUNK - 1, 0), 0, 0))
    mix_above = pl.BlockSpec((1, rows, lanes), lambda i: (jnp.minimum((i + 1) * CHUNK, depth - 1), 0, 0))
    gas_next, local, ends = pl.pallas_call(
        energy_kernel,
        grid=(steps,),
        out_shape=[
            shape(count + 1, depth, rows, lanes),
            shape(depth * rows, lanes),
            shape(2 * rows + 8, lanes),
        ],
        in_specs=[
            stack(2, 0), stack(1, count), below_of(1, count), above_of(1, count),
            planes, mix_below, mix_above, planes, side, side,
            fixed(*block_inverse.shape), fixed(*line_coupling.shape),
            tops, tops, edges, edges, sides, sides,
            side, side, edge, edge, mix_sides, mix_sides, ANY,
        ],
        out_specs=[stack(1, count), fixed(depth * rows, lanes), fixed(2 * rows + 8, lanes)],
        scratch_shapes=[pltpu.VMEM((depth * rows, lanes), F32)],
        input_output_aliases={24: 0},
        compiler_params=params(),
    )(
        gas_state, gas_state, gas_state, gas_state, mix, mix, mix, solids_temp, exchange_rate, column_flags,
        block_inverse, line_coupling, zlo, zhi, xlo, xhi, ylo, yhi, *mix_halos, gas_next,
    )
    slots = pl.pallas_call(
        share_kernel,
        out_shape=shape(segments, 2 * rows + 8, lanes),
        in_specs=[ANY],
        out_specs=ANY,
        scratch_shapes=[pltpu.SemaphoreType.DMA(()), pltpu.SemaphoreType.DMA((segments,)), pltpu.SemaphoreType.DMA((segments,))],
        compiler_params=pltpu.CompilerParams(collective_id=2, has_side_effects=True, vmem_limit_bytes=63 * 1024 * 1024),
    )(ends)
    part = 2 * CHUNK
    solved = pl.pallas_call(
        finish_kernel,
        out_shape=shape(depth * rows, lanes),
        grid=(depth // part,),
        in_specs=[
            fixed(segments, 2 * rows + 8, lanes),
            pl.BlockSpec((part * rows, lanes), lambda i: (i, 0)),
            pl.BlockSpec((part, depth), lambda i: (i, 0)),
        ],
        out_specs=pl.BlockSpec((part * rows, lanes), lambda i: (i, 0)),
        compiler_params=params(),
    )(slots, local, block_inverse)
    return (gas_next, solved.reshape(depth, rows, lanes))


def solution(mesh):
    in_specs = (
        P(None, "seg", "gx", "gy"),
        P("seg", "gx", "gy"),
        P("gx", "gy"),
        P("gx", "gy"),
        P("seg", None),
        P("seg", None),
    )
    out_specs = (P(None, "seg", "gx", "gy"), P("seg", "gx", "gy"))
    return jax.shard_map(body, mesh=mesh, in_specs=in_specs, out_specs=out_specs, check_vma=False)
```

```python
import jax
import jax.numpy as jnp
from jax import lax
from jax.experimental import pallas as pl
from jax.experimental.pallas import tpu as pltpu
from jax.sharding import PartitionSpec as P

diffusion = (0.1, 0.08, 0.12, 0.09, 0.11, 0.07)
stoich = (-1.0, -0.5, 1.0, 0.5, 0.25, 0.75)
rate_const = 0.3
upwind = 0.25
cond_base = 0.04
cond_slope = 0.3
heat_release = 0.5
lateral = 0.1
loss_table = (0.0, 0.3, 0.0, 0.1)
feed_table = (0.0, 0.0, 0.4, 0.0)
highest = lax.Precision.HIGHEST


MESH = pl.DeviceIdType.MESH
ANY = pl.BlockSpec(memory_space=pl.ANY)
F32 = jnp.float32
CHUNK = 16


def shape(*dims):
    return jax.ShapeDtypeStruct(dims, F32)


def params():
    return pltpu.CompilerParams(vmem_limit_bytes=63 * 1024 * 1024)


def iotas(rows, lanes):
    row = lax.broadcasted_iota(jnp.int32, (rows, lanes), 0)
    lane = lax.broadcasted_iota(jnp.int32, (rows, lanes), 1)
    return row, lane


def pack_columns(packed, plane, k, lane):
    lanes = plane.shape[1]
    moved = pltpu.roll(plane, 2 * k, 1) if k else plane
    ours = (lane == 2 * k) | (lane == (2 * k - 1) % lanes)
    return jnp.where(ours, moved, packed)


def page_of(step, lanes):
    per_page = lanes // (2 * CHUNK)
    return step // per_page, lax.rem(step, per_page) * (2 * CHUNK)


def merge_pages(low, high, lane):
    lanes = low.shape[1]
    return jnp.where(lane % 2 == 0, pltpu.roll(low, 1, 1), pltpu.roll(high, lanes - 1, 1))


def chunk_halo(low, high, step, lane):
    lanes = low.shape[1]
    _, offset = page_of(step, lanes)
    return pltpu.roll(merge_pages(low, high, lane), lax.rem(lanes - offset, lanes), 1)


def shifted(plane, row, lane, k, xlo, xhi, halo):
    rows, lanes = plane.shape
    west = jnp.where(row == 0, xlo, pltpu.roll(plane, 1, 0))
    east = jnp.where(row == rows - 1, xhi, pltpu.roll(plane, rows - 1, 0))
    column = pltpu.roll(halo, lanes - 2 * k, 1) if k else halo
    south = jnp.where(lane == 0, column, pltpu.roll(plane, 1, 1))
    north = jnp.where(lane == lanes - 1, column, pltpu.roll(plane, lanes - 1, 1))
    return west, east, south, north


def pack_field(read, field, chunk, x_first, x_last, y_pair):
    rows, lanes = y_pair.shape[2:]
    _, lane = iotas(rows, lanes)
    packed = jnp.zeros((rows, lanes), F32)
    for k in range(CHUNK):
        z = chunk * CHUNK + k
        plane = read(z)
        packed = pack_columns(packed, plane, k, lane)
        x_first[field, z : z + 1] = plane[0:1]
        x_last[field, z : z + 1] = plane[rows - 1 : rows]
    per_page = lanes // (2 * CHUNK)
    page, offset = chunk // per_page, chunk % per_page * (2 * CHUNK)
    moved = pltpu.roll(packed, offset, 1) if offset else packed
    y_pair[page, field] = moved if offset == 0 else y_pair[page, field] + moved


def pack_swap_kernel(
    gas, temp, zlo, zhi, xlo, xhi, ylo, yhi,
    gas_held, temp_held, x_first, x_last, y_pair, x_blank, z_blank, y_blank, load_sem, zero_sem, send_sem, recv_sem,
):
    fields, depth = gas.shape[:2]
    loads = []
    for chunk in range(depth // CHUNK):
        span = pl.ds(chunk * CHUNK, CHUNK)
        loads.append(
            (
                pltpu.make_async_copy(gas.at[:, span], gas_held.at[:, span], load_sem.at[2 * chunk]),
                pltpu.make_async_copy(temp.at[span], temp_held.at[span], load_sem.at[2 * chunk + 1]),
            )
        )
    for pair in loads:
        for load in pair:
            load.start()

    def prepare():
        for chunk, pair in enumerate(loads):
            for load in pair:
                load.wait()

            def one(field, carry, chunk=chunk):
                pack_field(lambda z: gas_held[field, z], field, chunk, x_first, x_last, y_pair)
                return carry

            lax.fori_loop(0, fields, one, 0)
            pack_field(lambda z: temp_held[z], fields, chunk, x_first, x_last, y_pair)

    swap_faces(
        (
            ("gx", x_first, x_last, xlo, xhi),
            ("seg", gas.at[:, 0], gas.at[:, depth - 1], zlo, zhi),
            ("gy", y_pair, y_pair, ylo, yhi),
        ),
        (x_blank, z_blank, y_blank),
        zero_sem,
        send_sem,
        recv_sem,
        prepare,
    )


def pack_swap(gas, temp, pages, ident):
    fields = gas.shape[0] + 1
    depth, rows, lanes = temp.shape
    top = shape(gas.shape[0], rows, lanes)
    side = shape(fields, depth, lanes)
    edge = shape(pages, fields, rows, lanes)
    sems = pltpu.SemaphoreType.DMA((6,))
    return pl.pallas_call(
        pack_swap_kernel,
        out_shape=[top, top, side, side, edge, edge],
        in_specs=[ANY] * 2,
        out_specs=[ANY] * 6,
        scratch_shapes=[
            pltpu.VMEM(held.shape, F32) for held in (gas, temp, side, side, edge, side, top, edge)
        ]
        + [pltpu.SemaphoreType.DMA((2 * (depth // CHUNK),)), sems, sems, sems],
        compiler_params=pltpu.CompilerParams(collective_id=ident, has_side_effects=True, vmem_limit_bytes=63 * 1024 * 1024),
    )(gas, temp)


def swap_faces(axes, blanks, zero_sem, send_sem, recv_sem, prepare=None):
    barrier = pltpu.get_barrier_semaphore()
    places = []
    for name, *_ in axes:
        here, count = lax.axis_index(name), lax.axis_size(name)
        places.append((here, here > 0, here < count - 1))
    for (name, *_), (here, down, up) in zip(axes, places):
        for exists, step in ((down, -1), (up, 1)):

            @pl.when(exists)
            def _(name=name, here=here, step=step):
                pl.semaphore_signal(barrier, inc=1, device_id={name: here + step}, device_id_type=MESH)

    peers = sum(exists.astype(jnp.int32) for _, *both in places for exists in both)
    pl.semaphore_wait(barrier, peers)

    plan = []
    for index, ((name, first, last, low, high), (here, down, up)) in enumerate(zip(axes, places)):
        to_up = pltpu.make_async_remote_copy(
            src_ref=last, dst_ref=low, send_sem=send_sem.at[2 * index], recv_sem=recv_sem.at[2 * index],
            device_id={name: here + 1}, device_id_type=MESH)
        to_down = pltpu.make_async_remote_copy(
            src_ref=first, dst_ref=high, send_sem=send_sem.at[2 * index + 1], recv_sem=recv_sem.at[2 * index + 1],
            device_id={name: here - 1}, device_id_type=MESH)
        plan.append((to_up, to_down, down, up, low, high))
    early = [entry for entry, axis in zip(plan, axes) if prepare is None or axis[0] == "seg"]
    for to_up, to_down, down, up, _, _ in early:
        pl.when(up)(to_up.start)
        pl.when(down)(to_down.start)
    for blank in blanks:
        blank[...] = jnp.zeros(blank.shape, F32)
    fills = []
    for index, (_, _, down, up, low, high) in enumerate(plan):
        for side, (exists, halo) in enumerate(((down, low), (up, high))):
            fill = pltpu.make_async_copy(blanks[index], halo, zero_sem.at[2 * index + side])
            fills.append((jnp.logical_not(exists), fill))
    for missing, fill in fills:
        pl.when(missing)(fill.start)
    if prepare is not None:
        prepare()
        for (to_up, to_down, down, up, _, _), axis in zip(plan, axes):
            if axis[0] != "seg":
                pl.when(up)(to_up.start)
                pl.when(down)(to_down.start)
    for to_up, to_down, down, up, low, high in plan:
        pl.when(up)(to_up.wait_send)
        pl.when(down)(to_down.wait_send)
        pl.when(down)(to_up.wait_recv)
        pl.when(up)(to_down.wait_recv)
    for missing, fill in fills:
        pl.when(missing)(fill.wait)


def swap_kernel(
    field, x_first, x_last, y_pair, zlo, zhi, xlo, xhi, ylo, yhi, x_blank, z_blank, y_blank, zero_sem, send_sem, recv_sem
):
    if len(field.shape) == 4:
        z_first, z_last = field.at[:, 0], field.at[:, field.shape[1] - 1]
    else:
        z_first, z_last = field.at[0], field.at[field.shape[0] - 1]
    swap_faces(
        (
            ("gx", x_first, x_last, xlo, xhi),
            ("seg", z_first, z_last, zlo, zhi),
            ("gy", y_pair, y_pair, ylo, yhi),
        ),
        (x_blank, z_blank, y_blank),
        zero_sem,
        send_sem,
        recv_sem,
    )


def swap(field, x_first, x_last, y_pair, ident):
    top = shape(*field.shape[:-3], *field.shape[-2:])
    side = shape(*x_first.shape)
    edge = shape(*y_pair.shape)
    sems = pltpu.SemaphoreType.DMA((6,))
    return pl.pallas_call(
        swap_kernel,
        out_shape=[top, top, side, side, edge, edge],
        in_specs=[ANY] * 4,
        out_specs=[ANY] * 6,
        scratch_shapes=[pltpu.VMEM(face.shape, F32) for face in (side, top, edge)] + [sems, sems, sems],
        compiler_params=pltpu.CompilerParams(collective_id=ident, has_side_effects=True, vmem_limit_bytes=63 * 1024 * 1024),
    )(field, x_first, x_last, y_pair)


def species_kernel(
    gas, before, after, zlo, zhi, xlo, xhi, ylo, yhi, new, mix_out, x_first, x_last, y_pair
):
    step, steps = pl.program_id(0), pl.num_programs(0)
    count, depth, rows, lanes = gas.shape
    row, lane = iotas(rows, lanes)
    at_bottom, at_top = step == 0, step == steps - 1

    @pl.when(step == 0)
    def _():
        y_pair[...] = jnp.zeros_like(y_pair)

    page, offset = page_of(step, lanes)
    packed = jnp.zeros((rows, lanes), F32)
    halos = [chunk_halo(ylo[page, s], yhi[page, s], step, lane) for s in range(count)]
    for k in range(depth):
        reaction = rate_const * gas[0, k] * gas[1, k]
        total = None
        for s in range(count):
            center = gas[s, k]
            below = gas[s, k - 1] if k > 0 else jnp.where(at_bottom, zlo[s], before[s, 0])
            above = gas[s, k + 1] if k < depth - 1 else jnp.where(at_top, zhi[s], after[s, 0])
            west, east, south, north = shifted(
                center, row, lane, k, xlo[s, k : k + 1], xhi[s, k : k + 1], halos[s]
            )
            beside = (below + above) + (west + east) + (south + north)
            value = (
                center
                + diffusion[s] * (beside - 6.0 * center)
                - upwind * (center - below)
                + stoich[s] * reaction
            )
            new[s, k] = value
            total = value if total is None else total + value
        mix = 0.5 * total
        mix_out[k] = mix
        packed = pack_columns(packed, mix, k, lane)
        x_first[k : k + 1] = mix[0:1]
        x_last[k : k + 1] = mix[rows - 1 : rows]
    y_pair[page] += pltpu.roll(packed, offset, 1)


def lookup(flags, table):
    result = jnp.zeros(flags.shape, F32)
    for value, entry in enumerate(table):
        result = result + jnp.where(flags == value, entry, 0.0)
    return result


def energy_kernel(
    pair, heat, heat_before, heat_after, mix, mix_before, mix_after, temp, exchange, flags, inverse, coupling,
    zlo, zhi, xlo, xhi, ylo, yhi, mzlo, mzhi, mxlo, mxhi, mylo, myhi, gas_in,
    heat_out, local, ends, source,
):
    step, steps = pl.program_id(0), pl.num_programs(0)
    depth, rows, lanes = temp.shape
    row, lane = iotas(rows, lanes)
    at_bottom, at_top = step == 0, step == steps - 1
    loss = lookup(flags[...], loss_table)
    feed = lookup(flags[...], feed_table)
    rate = exchange[...]
    page, _ = page_of(step, lanes)
    heat_halo = chunk_halo(ylo[page, 6], yhi[page, 6], step, lane)
    temp_halo = chunk_halo(ylo[page, 7], yhi[page, 7], step, lane)
    mix_halo = chunk_halo(mylo[page], myhi[page], step, lane)
    for k in range(depth):
        z = step * depth + k
        reaction = rate_const * pair[0, k] * pair[1, k]
        heat_mid, mix_mid, temp_mid = heat[0, k], mix[k], temp[k]
        heat_below = heat[0, k - 1] if k > 0 else jnp.where(at_bottom, zlo[6], heat_before[0, 0])
        heat_above = heat[0, k + 1] if k < depth - 1 else jnp.where(at_top, zhi[6], heat_after[0, 0])
        mix_below = mix[k - 1] if k > 0 else jnp.where(at_bottom, mzlo[...], mix_before[0])
        mix_above = mix[k + 1] if k < depth - 1 else jnp.where(at_top, mzhi[...], mix_after[0])
        one = slice(k, k + 1)
        heats = (heat_below, heat_above) + shifted(
            heat_mid, row, lane, k, xlo[6, one], xhi[6, one], heat_halo
        )
        mixes = (mix_below, mix_above) + shifted(
            mix_mid, row, lane, k, mxlo[one], mxhi[one], mix_halo
        )
        temps = shifted(temp_mid, row, lane, k, xlo[7, one], xhi[7, one], temp_halo)
        cond_mid = cond_base + cond_slope * mix_mid
        flux = None
        for heat_near, mix_near in zip(heats, mixes):
            part = (cond_mid + (cond_base + cond_slope * mix_near)) * (heat_near - heat_mid)
            flux = part if flux is None else flux + part
        heat_new = heat_mid + 0.5 * flux + heat_release * reaction - loss * heat_mid + feed
        heat_out[0, k] = heat_new
        beside = (temps[0] + temps[1]) + (temps[2] + temps[3])
        planes = temp_mid + lateral * (beside - 4.0 * temp_mid) + rate * (heat_new - temp_mid)
        source[pl.ds(pl.multiple_of(z * rows, rows), rows), :] = planes

    @pl.when(at_top)
    def _():
        size = inverse.shape[0]
        group = 4
        for start in range(0, rows, group):
            right = jnp.concatenate(
                [source[pl.ds(start + j, size, stride=rows), :] for j in range(group)], axis=1
            )
            result = jnp.dot(inverse[...], right, precision=highest, preferred_element_type=F32)
            for j in range(group):
                local[pl.ds(start + j, size, stride=rows), :] = result[:, j * lanes : (j + 1) * lanes]
        ends[0:rows] = local[0:rows]
        ends[rows : 2 * rows] = local[(size - 1) * rows : size * rows]
        scalars = (
            inverse[0:1, 0:1],
            inverse[size - 1 : size, 0:1],
            inverse[0:1, size - 1 : size],
            inverse[size - 1 : size, size - 1 : size],
            coupling[0:1, 0:1],
            coupling[0:1, 1:2],
        )
        for index, scalar in enumerate(scalars):
            ends[2 * rows + index : 2 * rows + index + 1] = jnp.broadcast_to(scalar, (1, lanes))
        ends[2 * rows + 6 : 2 * rows + 8] = jnp.zeros((2, lanes), F32)


def share_kernel(ends, slots, own_sem, send_sem, recv_sem):
    here, count = lax.axis_index("seg"), lax.axis_size("seg")
    barrier = pltpu.get_barrier_semaphore()
    for step in range(1, count):
        pl.semaphore_signal(
            barrier, inc=1, device_id={"seg": lax.rem(here + step, count)}, device_id_type=MESH)
    pl.semaphore_wait(barrier, count - 1)
    copies = [
        pltpu.make_async_remote_copy(
            src_ref=ends, dst_ref=slots.at[step], send_sem=send_sem.at[step], recv_sem=recv_sem.at[step],
            device_id={"seg": lax.rem(here + step, count)}, device_id_type=MESH)
        for step in range(1, count)
    ]
    for copy in copies:
        copy.start()
    own = pltpu.make_async_copy(ends, slots.at[0], own_sem)
    own.start()
    own.wait()
    for copy in copies:
        copy.wait()


def finish_kernel(slots, local, inverse, out):
    count, total_rows, lanes = slots.shape
    rows = (total_rows - 8) // 2
    size, width = inverse.shape
    here = lax.axis_index("seg")
    held = [slots[lax.rem(here - s + count, count)] for s in range(count)]
    p_lines, q_lines = [], []
    for s in range(count):
        y_first, y_last = held[s][0:rows], held[s][rows : 2 * rows]
        b00, b90, b09, b99, lower, upper = (held[s][2 * rows + j : 2 * rows + j + 1] for j in range(6))
        p_gain = upper * b09 if s < count - 1 else jnp.zeros_like(upper)
        q_gain = upper * b99 if s < count - 1 else jnp.zeros_like(upper)
        p_const, q_const = y_first, y_last
        if s > 0:
            before_const, before_gain = q_lines[-1]
            into_p, into_q = lower * b00, lower * b90
            scale = 1.0 / (1.0 - into_p * before_gain)
            p_const = (y_first + into_p * before_const) * scale
            p_gain = p_gain * scale
            link = into_q * before_gain
            q_const = y_last + into_q * before_const + link * p_const
            q_gain = q_gain + link * p_gain
        p_lines.append((p_const, p_gain))
        q_lines.append((q_const, q_gain))
    firsts, lasts = [None] * count, [None] * count
    above = jnp.zeros((rows, lanes), F32)
    for s in reversed(range(count)):
        firsts[s] = p_lines[s][0] + p_lines[s][1] * above
        lasts[s] = q_lines[s][0] + q_lines[s][1] * above
        above = firsts[s]
    q_near = jnp.zeros((rows, lanes), F32)
    p_near = jnp.zeros((rows, lanes), F32)
    for s in range(count):
        if s > 0:
            q_near = jnp.where(here == s, lasts[s - 1], q_near)
        if s < count - 1:
            p_near = jnp.where(here == s, firsts[s + 1], p_near)
    mine = slots[0]
    q_near = mine[2 * rows + 4 : 2 * rows + 5] * q_near
    p_near = mine[2 * rows + 5 : 2 * rows + 6] * p_near
    for z in range(size):
        low = jnp.broadcast_to(inverse[z : z + 1, 0:1], (1, lanes))
        high = jnp.broadcast_to(inverse[z : z + 1, width - 1 : width], (1, lanes))
        block = slice(z * rows, (z + 1) * rows)
        out[block] = local[block] + q_near * low + p_near * high


def body(gas_state, solids_temp, exchange_rate, column_flags, block_inverse, line_coupling):
    count = gas_state.shape[0] - 1
    depth, rows, lanes = solids_temp.shape
    segments = lax.axis_size("seg")
    steps = depth // CHUNK
    fields = count + 2

    def fixed(*dims):
        return pl.BlockSpec(dims, lambda i: (0,) * len(dims))

    def stack(number, start):
        return pl.BlockSpec((number, CHUNK, rows, lanes), lambda i: (start, i, 0, 0))

    def below_of(number, start):
        return pl.BlockSpec(
            (number, 1, rows, lanes), lambda i: (start, jnp.maximum(i * CHUNK - 1, 0), 0, 0))

    def above_of(number, start):
        return pl.BlockSpec(
            (number, 1, rows, lanes), lambda i: (start, jnp.minimum((i + 1) * CHUNK, depth - 1), 0, 0))

    planes = pl.BlockSpec((CHUNK, rows, lanes), lambda i: (i, 0, 0))
    edge = pl.BlockSpec((CHUNK, lanes), lambda i: (i, 0))
    edges = pl.BlockSpec((fields, CHUNK, lanes), lambda i: (0, i, 0))
    pages = -(-2 * depth // lanes)
    sides = fixed(pages, fields, rows, lanes)
    tops = fixed(count + 1, rows, lanes)
    side = fixed(rows, lanes)
    mix_sides = fixed(pages, rows, lanes)

    zlo, zhi, xlo, xhi, ylo, yhi = pack_swap(gas_state, solids_temp, pages, 0)
    gas_next, mix, mx_first, mx_last, my_pair = pl.pallas_call(
        species_kernel,
        grid=(steps,),
        out_shape=[shape(count + 1, depth, rows, lanes), shape(depth, rows, lanes)]
        + [shape(depth, lanes)] * 2
        + [shape(pages, rows, lanes)],
        in_specs=[stack(count, 0), below_of(count, 0), above_of(count, 0), tops, tops, edges, edges, sides, sides],
        out_specs=[stack(count, 0), planes, edge, edge, mix_sides],
        compiler_params=params(),
    )(gas_state, gas_state, gas_state, zlo, zhi, xlo, xhi, ylo, yhi)
    mix_halos = swap(mix, mx_first, mx_last, my_pair, 1)
    mix_below = pl.BlockSpec((1, rows, lanes), lambda i: (jnp.maximum(i * CHUNK - 1, 0), 0, 0))
    mix_above = pl.BlockSpec((1, rows, lanes), lambda i: (jnp.minimum((i + 1) * CHUNK, depth - 1), 0, 0))
    gas_next, local, ends = pl.pallas_call(
        energy_kernel,
        grid=(steps,),
        out_shape=[
            shape(count + 1, depth, rows, lanes),
            shape(depth * rows, lanes),
            shape(2 * rows + 8, lanes),
        ],
        in_specs=[
            stack(2, 0), stack(1, count), below_of(1, count), above_of(1, count),
            planes, mix_below, mix_above, planes, side, side,
            fixed(*block_inverse.shape), fixed(*line_coupling.shape),
            tops, tops, edges, edges, sides, sides,
            side, side, edge, edge, mix_sides, mix_sides, ANY,
        ],
        out_specs=[stack(1, count), fixed(depth * rows, lanes), fixed(2 * rows + 8, lanes)],
        scratch_shapes=[pltpu.VMEM((depth * rows, lanes), F32)],
        input_output_aliases={24: 0},
        compiler_params=params(),
    )(
        gas_state, gas_state, gas_state, gas_state, mix, mix, mix, solids_temp, exchange_rate, column_flags,
        block_inverse, line_coupling, zlo, zhi, xlo, xhi, ylo, yhi, *mix_halos, gas_next,
    )
    slots = pl.pallas_call(
        share_kernel,
        out_shape=shape(segments, 2 * rows + 8, lanes),
        in_specs=[ANY],
        out_specs=ANY,
        scratch_shapes=[pltpu.SemaphoreType.DMA(()), pltpu.SemaphoreType.DMA((segments,)), pltpu.SemaphoreType.DMA((segments,))],
        compiler_params=pltpu.CompilerParams(collective_id=2, has_side_effects=True, vmem_limit_bytes=63 * 1024 * 1024),
    )(ends)
    part = 2 * CHUNK
    solved = pl.pallas_call(
        finish_kernel,
        out_shape=shape(depth * rows, lanes),
        grid=(depth // part,),
        in_specs=[
            fixed(segments, 2 * rows + 8, lanes),
            pl.BlockSpec((part * rows, lanes), lambda i: (i, 0)),
            pl.BlockSpec((part, depth), lambda i: (i, 0)),
        ],
        out_specs=pl.BlockSpec((part * rows, lanes), lambda i: (i, 0)),
        compiler_params=params(),
    )(slots, local, block_inverse)
    return (gas_next, solved.reshape(depth, rows, lanes))


def solution(mesh):
    in_specs = (
        P(None, "seg", "gx", "gy"),
        P("seg", "gx", "gy"),
        P("gx", "gy"),
        P("gx", "gy"),
        P("seg", None),
        P("seg", None),
    )
    out_specs = (P(None, "seg", "gx", "gy"), P("seg", "gx", "gy"))
    return jax.shard_map(body, mesh=mesh, in_specs=in_specs, out_specs=out_specs, check_vma=False)
```

```python
import jax
import jax.numpy as jnp
from jax import lax
from jax.experimental import pallas as pl
from jax.experimental.pallas import tpu as pltpu
from jax.sharding import PartitionSpec as P

diffusion = (0.1, 0.08, 0.12, 0.09, 0.11, 0.07)
stoich = (-1.0, -0.5, 1.0, 0.5, 0.25, 0.75)
rate_const = 0.3
upwind = 0.25
cond_base = 0.04
cond_slope = 0.3
heat_release = 0.5
lateral = 0.1
loss_table = (0.0, 0.3, 0.0, 0.1)
feed_table = (0.0, 0.0, 0.4, 0.0)
highest = lax.Precision.HIGHEST


MESH = pl.DeviceIdType.MESH
ANY = pl.BlockSpec(memory_space=pl.ANY)
F32 = jnp.float32
CHUNK = 16


def shape(*dims):
    return jax.ShapeDtypeStruct(dims, F32)


def params():
    return pltpu.CompilerParams(vmem_limit_bytes=63 * 1024 * 1024)


def iotas(rows, lanes):
    row = lax.broadcasted_iota(jnp.int32, (rows, lanes), 0)
    lane = lax.broadcasted_iota(jnp.int32, (rows, lanes), 1)
    return row, lane


def pack_columns(packed, plane, k, lane):
    lanes = plane.shape[1]
    moved = pltpu.roll(plane, 2 * k, 1) if k else plane
    ours = (lane == 2 * k) | (lane == (2 * k - 1) % lanes)
    return jnp.where(ours, moved, packed)


def page_of(step, lanes):
    per_page = lanes // (2 * CHUNK)
    return step // per_page, lax.rem(step, per_page) * (2 * CHUNK)


def merge_pages(low, high, lane):
    lanes = low.shape[1]
    return jnp.where(lane % 2 == 0, pltpu.roll(low, 1, 1), pltpu.roll(high, lanes - 1, 1))


def chunk_halo(low, high, step, lane):
    lanes = low.shape[1]
    _, offset = page_of(step, lanes)
    return pltpu.roll(merge_pages(low, high, lane), lax.rem(lanes - offset, lanes), 1)


def shifted(plane, row, lane, k, xlo, xhi, halo, less=None, more=None):
    rows, lanes = plane.shape
    less = pltpu.roll(plane, 1, 0) if less is None else less
    more = pltpu.roll(plane, rows - 1, 0) if more is None else more
    west = jnp.where(row == 0, xlo, less)
    east = jnp.where(row == rows - 1, xhi, more)
    column = pltpu.roll(halo, lanes - 2 * k, 1) if k else halo
    south = jnp.where(lane == 0, column, pltpu.roll(plane, 1, 1))
    north = jnp.where(lane == lanes - 1, column, pltpu.roll(plane, lanes - 1, 1))
    return west, east, south, north


def pack_field(held, field, chunk, x_first, x_last, y_pair):
    rows, lanes = y_pair.shape[2:]
    _, lane = iotas(rows, lanes)
    packed = jnp.zeros((rows, lanes), F32)
    for k in range(CHUNK):
        z = chunk * CHUNK + k
        packed = pack_columns(packed, held[pl.ds(z * rows, rows), :], k, lane)
    start, span = chunk * CHUNK, pl.ds(chunk * CHUNK, CHUNK)
    x_first[field, span] = held[pl.ds(start * rows, CHUNK, stride=rows), :]
    x_last[field, span] = held[pl.ds(start * rows + rows - 1, CHUNK, stride=rows), :]
    per_page = lanes // (2 * CHUNK)
    page, offset = chunk // per_page, chunk % per_page * (2 * CHUNK)
    moved = pltpu.roll(packed, offset, 1) if offset else packed
    y_pair[page, field] = moved if offset == 0 else y_pair[page, field] + moved


def pack_swap_kernel(
    gas, temp, zlo, zhi, xlo, xhi, ylo, yhi,
    gas_held, temp_held, x_first, x_last, y_pair, x_blank, z_blank, y_blank, load_sem, zero_sem, send_sem, recv_sem,
):
    fields, depth, rows = gas.shape[0], x_first.shape[1], y_pair.shape[2]
    loads = []
    for chunk in range(depth // CHUNK):
        span = pl.ds(chunk * CHUNK * rows, CHUNK * rows)
        loads.append(
            (
                pltpu.make_async_copy(gas.at[:, span], gas_held.at[:, span], load_sem.at[2 * chunk]),
                pltpu.make_async_copy(temp.at[span], temp_held.at[span], load_sem.at[2 * chunk + 1]),
            )
        )
    for pair in loads:
        for load in pair:
            load.start()

    def prepare():
        for chunk, pair in enumerate(loads):
            for load in pair:
                load.wait()

            def one(field, carry, chunk=chunk):
                pack_field(gas_held.at[field], field, chunk, x_first, x_last, y_pair)
                return carry

            lax.fori_loop(0, fields, one, 0)
            pack_field(temp_held, fields, chunk, x_first, x_last, y_pair)

    swap_faces(
        (
            ("gx", x_first, x_last, xlo, xhi),
            ("seg", gas.at[:, pl.ds(0, rows)], gas.at[:, pl.ds((depth - 1) * rows, rows)], zlo, zhi),
            ("gy", y_pair, y_pair, ylo, yhi),
        ),
        (x_blank, z_blank, y_blank),
        zero_sem,
        send_sem,
        recv_sem,
        prepare,
    )


def pack_swap(gas, temp, pages, ident):
    fields = gas.shape[0] + 1
    depth, rows, lanes = temp.shape
    top = shape(gas.shape[0], rows, lanes)
    side = shape(fields, depth, lanes)
    edge = shape(pages, fields, rows, lanes)
    sems = pltpu.SemaphoreType.DMA((6,))
    flat_gas = gas.reshape(gas.shape[0], depth * rows, lanes)
    flat_temp = temp.reshape(depth * rows, lanes)
    return pl.pallas_call(
        pack_swap_kernel,
        out_shape=[top, top, side, side, edge, edge],
        in_specs=[ANY] * 2,
        out_specs=[ANY] * 6,
        scratch_shapes=[
            pltpu.VMEM(held.shape, F32) for held in (flat_gas, flat_temp, side, side, edge, side, top, edge)
        ]
        + [pltpu.SemaphoreType.DMA((2 * (depth // CHUNK),)), sems, sems, sems],
        compiler_params=pltpu.CompilerParams(collective_id=ident, has_side_effects=True, vmem_limit_bytes=63 * 1024 * 1024),
    )(flat_gas, flat_temp)


def swap_faces(axes, blanks, zero_sem, send_sem, recv_sem, prepare=None):
    barrier = pltpu.get_barrier_semaphore()
    places = []
    for name, *_ in axes:
        here, count = lax.axis_index(name), lax.axis_size(name)
        places.append((here, here > 0, here < count - 1))
    for (name, *_), (here, down, up) in zip(axes, places):
        for exists, step in ((down, -1), (up, 1)):

            @pl.when(exists)
            def _(name=name, here=here, step=step):
                pl.semaphore_signal(barrier, inc=1, device_id={name: here + step}, device_id_type=MESH)

    peers = sum(exists.astype(jnp.int32) for _, *both in places for exists in both)
    pl.semaphore_wait(barrier, peers)

    plan = []
    for index, ((name, first, last, low, high), (here, down, up)) in enumerate(zip(axes, places)):
        to_up = pltpu.make_async_remote_copy(
            src_ref=last, dst_ref=low, send_sem=send_sem.at[2 * index], recv_sem=recv_sem.at[2 * index],
            device_id={name: here + 1}, device_id_type=MESH)
        to_down = pltpu.make_async_remote_copy(
            src_ref=first, dst_ref=high, send_sem=send_sem.at[2 * index + 1], recv_sem=recv_sem.at[2 * index + 1],
            device_id={name: here - 1}, device_id_type=MESH)
        plan.append((to_up, to_down, down, up, low, high))
    early = [entry for entry, axis in zip(plan, axes) if prepare is None or axis[0] == "seg"]
    for to_up, to_down, down, up, _, _ in early:
        pl.when(up)(to_up.start)
        pl.when(down)(to_down.start)
    for blank in blanks:
        blank[...] = jnp.zeros(blank.shape, F32)
    fills = []
    for index, (_, _, down, up, low, high) in enumerate(plan):
        for side, (exists, halo) in enumerate(((down, low), (up, high))):
            fill = pltpu.make_async_copy(blanks[index], halo, zero_sem.at[2 * index + side])
            fills.append((jnp.logical_not(exists), fill))
    for missing, fill in fills:
        pl.when(missing)(fill.start)
    if prepare is not None:
        prepare()
        for (to_up, to_down, down, up, _, _), axis in zip(plan, axes):
            if axis[0] != "seg":
                pl.when(up)(to_up.start)
                pl.when(down)(to_down.start)
    for to_up, to_down, down, up, low, high in plan:
        pl.when(up)(to_up.wait_send)
        pl.when(down)(to_down.wait_send)
        pl.when(down)(to_up.wait_recv)
        pl.when(up)(to_down.wait_recv)
    for missing, fill in fills:
        pl.when(missing)(fill.wait)


def swap_kernel(
    field, x_first, x_last, y_pair, zlo, zhi, xlo, xhi, ylo, yhi, x_blank, z_blank, y_blank, zero_sem, send_sem, recv_sem
):
    if len(field.shape) == 4:
        z_first, z_last = field.at[:, 0], field.at[:, field.shape[1] - 1]
    else:
        z_first, z_last = field.at[0], field.at[field.shape[0] - 1]
    swap_faces(
        (
            ("gx", x_first, x_last, xlo, xhi),
            ("seg", z_first, z_last, zlo, zhi),
            ("gy", y_pair, y_pair, ylo, yhi),
        ),
        (x_blank, z_blank, y_blank),
        zero_sem,
        send_sem,
        recv_sem,
    )


def swap(field, x_first, x_last, y_pair, ident):
    top = shape(*field.shape[:-3], *field.shape[-2:])
    side = shape(*x_first.shape)
    edge = shape(*y_pair.shape)
    sems = pltpu.SemaphoreType.DMA((6,))
    return pl.pallas_call(
        swap_kernel,
        out_shape=[top, top, side, side, edge, edge],
        in_specs=[ANY] * 4,
        out_specs=[ANY] * 6,
        scratch_shapes=[pltpu.VMEM(face.shape, F32) for face in (side, top, edge)] + [sems, sems, sems],
        compiler_params=pltpu.CompilerParams(collective_id=ident, has_side_effects=True, vmem_limit_bytes=63 * 1024 * 1024),
    )(field, x_first, x_last, y_pair)


def species_kernel(
    gas, before, after, zlo, zhi, xlo, xhi, ylo, yhi, new, mix_out, x_first, x_last, y_pair
):
    step, steps = pl.program_id(0), pl.num_programs(0)
    count, depth, rows, lanes = new.shape
    row, lane = iotas(rows, lanes)
    at_bottom, at_top = step == 0, step == steps - 1

    @pl.when(step == 0)
    def _():
        y_pair[...] = jnp.zeros_like(y_pair)

    page, offset = page_of(step, lanes)
    packed = jnp.zeros((rows, lanes), F32)
    halos = [chunk_halo(ylo[page, s], yhi[page, s], step, lane) for s in range(count)]
    for k in range(depth):
        here = slice(k * rows, (k + 1) * rows)
        reaction = rate_const * gas[0, here] * gas[1, here]
        total = None
        for s in range(count):
            center = gas[s, here]
            down, up = slice((k - 1) * rows, k * rows), slice((k + 1) * rows, (k + 2) * rows)
            below = gas[s, down] if k > 0 else jnp.where(at_bottom, zlo[s], before[s])
            above = gas[s, up] if k < depth - 1 else jnp.where(at_top, zhi[s], after[s])
            less = gas[s, k * rows - 1 : (k + 1) * rows - 1] if k > 0 else None
            more = gas[s, k * rows + 1 : (k + 1) * rows + 1] if k < depth - 1 else None
            west, east, south, north = shifted(
                center, row, lane, k, xlo[s, k : k + 1], xhi[s, k : k + 1], halos[s], less, more
            )
            beside = (below + above) + (west + east) + (south + north)
            value = (
                center
                + diffusion[s] * (beside - 6.0 * center)
                - upwind * (center - below)
                + stoich[s] * reaction
            )
            new[s, k] = value
            total = value if total is None else total + value
        mix = 0.5 * total
        mix_out[k] = mix
        packed = pack_columns(packed, mix, k, lane)
        x_first[k : k + 1] = mix[0:1]
        x_last[k : k + 1] = mix[rows - 1 : rows]
    y_pair[page] += pltpu.roll(packed, offset, 1)


def lookup(flags, table):
    result = jnp.zeros(flags.shape, F32)
    for value, entry in enumerate(table):
        result = result + jnp.where(flags == value, entry, 0.0)
    return result


def energy_kernel(
    pair, heat, heat_before, heat_after, mix, mix_before, mix_after, temp, exchange, flags, inverse, coupling,
    zlo, zhi, xlo, xhi, ylo, yhi, mzlo, mzhi, mxlo, mxhi, mylo, myhi, gas_in,
    heat_out, local, ends, source,
):
    step, steps = pl.program_id(0), pl.num_programs(0)
    depth, rows, lanes = temp.shape
    row, lane = iotas(rows, lanes)
    at_bottom, at_top = step == 0, step == steps - 1
    loss = lookup(flags[...], loss_table)
    feed = lookup(flags[...], feed_table)
    rate = exchange[...]
    page, _ = page_of(step, lanes)
    heat_halo = chunk_halo(ylo[page, 6], yhi[page, 6], step, lane)
    temp_halo = chunk_halo(ylo[page, 7], yhi[page, 7], step, lane)
    mix_halo = chunk_halo(mylo[page], myhi[page], step, lane)
    for k in range(depth):
        z = step * depth + k
        reaction = rate_const * pair[0, k] * pair[1, k]
        heat_mid, mix_mid, temp_mid = heat[0, k], mix[k], temp[k]
        heat_below = heat[0, k - 1] if k > 0 else jnp.where(at_bottom, zlo[6], heat_before[0, 0])
        heat_above = heat[0, k + 1] if k < depth - 1 else jnp.where(at_top, zhi[6], heat_after[0, 0])
        mix_below = mix[k - 1] if k > 0 else jnp.where(at_bottom, mzlo[...], mix_before[0])
        mix_above = mix[k + 1] if k < depth - 1 else jnp.where(at_top, mzhi[...], mix_after[0])
        one = slice(k, k + 1)
        heats = (heat_below, heat_above) + shifted(
            heat_mid, row, lane, k, xlo[6, one], xhi[6, one], heat_halo
        )
        mixes = (mix_below, mix_above) + shifted(
            mix_mid, row, lane, k, mxlo[one], mxhi[one], mix_halo
        )
        temps = shifted(temp_mid, row, lane, k, xlo[7, one], xhi[7, one], temp_halo)
        cond_mid = cond_base + cond_slope * mix_mid
        flux = None
        for heat_near, mix_near in zip(heats, mixes):
            part = (cond_mid + (cond_base + cond_slope * mix_near)) * (heat_near - heat_mid)
            flux = part if flux is None else flux + part
        heat_new = heat_mid + 0.5 * flux + heat_release * reaction - loss * heat_mid + feed
        heat_out[0, k] = heat_new
        beside = (temps[0] + temps[1]) + (temps[2] + temps[3])
        planes = temp_mid + lateral * (beside - 4.0 * temp_mid) + rate * (heat_new - temp_mid)
        source[pl.ds(pl.multiple_of(z * rows, rows), rows), :] = planes

    @pl.when(at_top)
    def _():
        size = inverse.shape[0]
        group = 4
        for start in range(0, rows, group):
            right = jnp.concatenate(
                [source[pl.ds(start + j, size, stride=rows), :] for j in range(group)], axis=1
            )
            result = jnp.dot(inverse[...], right, precision=highest, preferred_element_type=F32)
            for j in range(group):
                local[pl.ds(start + j, size, stride=rows), :] = result[:, j * lanes : (j + 1) * lanes]
        ends[0:rows] = local[0:rows]
        ends[rows : 2 * rows] = local[(size - 1) * rows : size * rows]
        scalars = (
            inverse[0:1, 0:1],
            inverse[size - 1 : size, 0:1],
            inverse[0:1, size - 1 : size],
            inverse[size - 1 : size, size - 1 : size],
            coupling[0:1, 0:1],
            coupling[0:1, 1:2],
        )
        for index, scalar in enumerate(scalars):
            ends[2 * rows + index : 2 * rows + index + 1] = jnp.broadcast_to(scalar, (1, lanes))
        ends[2 * rows + 6 : 2 * rows + 8] = jnp.zeros((2, lanes), F32)


def share_kernel(ends, slots, own_sem, send_sem, recv_sem):
    here, count = lax.axis_index("seg"), lax.axis_size("seg")
    barrier = pltpu.get_barrier_semaphore()
    for step in range(1, count):
        pl.semaphore_signal(
            barrier, inc=1, device_id={"seg": lax.rem(here + step, count)}, device_id_type=MESH)
    pl.semaphore_wait(barrier, count - 1)
    copies = [
        pltpu.make_async_remote_copy(
            src_ref=ends, dst_ref=slots.at[step], send_sem=send_sem.at[step], recv_sem=recv_sem.at[step],
            device_id={"seg": lax.rem(here + step, count)}, device_id_type=MESH)
        for step in range(1, count)
    ]
    for copy in copies:
        copy.start()
    own = pltpu.make_async_copy(ends, slots.at[0], own_sem)
    own.start()
    own.wait()
    for copy in copies:
        copy.wait()


def finish_kernel(slots, local, inverse, out):
    count, total_rows, lanes = slots.shape
    rows = (total_rows - 8) // 2
    size, width = inverse.shape
    here = lax.axis_index("seg")
    held = [slots[lax.rem(here - s + count, count)] for s in range(count)]
    p_lines, q_lines = [], []
    for s in range(count):
        y_first, y_last = held[s][0:rows], held[s][rows : 2 * rows]
        b00, b90, b09, b99, lower, upper = (held[s][2 * rows + j : 2 * rows + j + 1] for j in range(6))
        p_gain = upper * b09 if s < count - 1 else jnp.zeros_like(upper)
        q_gain = upper * b99 if s < count - 1 else jnp.zeros_like(upper)
        p_const, q_const = y_first, y_last
        if s > 0:
            before_const, before_gain = q_lines[-1]
            into_p, into_q = lower * b00, lower * b90
            scale = 1.0 / (1.0 - into_p * before_gain)
            p_const = (y_first + into_p * before_const) * scale
            p_gain = p_gain * scale
            link = into_q * before_gain
            q_const = y_last + into_q * before_const + link * p_const
            q_gain = q_gain + link * p_gain
        p_lines.append((p_const, p_gain))
        q_lines.append((q_const, q_gain))
    firsts, lasts = [None] * count, [None] * count
    above = jnp.zeros((rows, lanes), F32)
    for s in reversed(range(count)):
        firsts[s] = p_lines[s][0] + p_lines[s][1] * above
        lasts[s] = q_lines[s][0] + q_lines[s][1] * above
        above = firsts[s]
    q_near = jnp.zeros((rows, lanes), F32)
    p_near = jnp.zeros((rows, lanes), F32)
    for s in range(count):
        if s > 0:
            q_near = jnp.where(here == s, lasts[s - 1], q_near)
        if s < count - 1:
            p_near = jnp.where(here == s, firsts[s + 1], p_near)
    mine = slots[0]
    q_near = mine[2 * rows + 4 : 2 * rows + 5] * q_near
    p_near = mine[2 * rows + 5 : 2 * rows + 6] * p_near
    for z in range(size):
        low = jnp.broadcast_to(inverse[z : z + 1, 0:1], (1, lanes))
        high = jnp.broadcast_to(inverse[z : z + 1, width - 1 : width], (1, lanes))
        block = slice(z * rows, (z + 1) * rows)
        out[block] = local[block] + q_near * low + p_near * high


def body(gas_state, solids_temp, exchange_rate, column_flags, block_inverse, line_coupling):
    count = gas_state.shape[0] - 1
    depth, rows, lanes = solids_temp.shape
    segments = lax.axis_size("seg")
    steps = depth // CHUNK
    fields = count + 2

    def fixed(*dims):
        return pl.BlockSpec(dims, lambda i: (0,) * len(dims))

    def stack(number, start):
        return pl.BlockSpec((number, CHUNK, rows, lanes), lambda i: (start, i, 0, 0))

    def below_of(number, start):
        return pl.BlockSpec(
            (number, 1, rows, lanes), lambda i: (start, jnp.maximum(i * CHUNK - 1, 0), 0, 0))

    def above_of(number, start):
        return pl.BlockSpec(
            (number, 1, rows, lanes), lambda i: (start, jnp.minimum((i + 1) * CHUNK, depth - 1), 0, 0))

    planes = pl.BlockSpec((CHUNK, rows, lanes), lambda i: (i, 0, 0))
    edge = pl.BlockSpec((CHUNK, lanes), lambda i: (i, 0))
    edges = pl.BlockSpec((fields, CHUNK, lanes), lambda i: (0, i, 0))
    pages = -(-2 * depth // lanes)
    sides = fixed(pages, fields, rows, lanes)
    tops = fixed(count + 1, rows, lanes)
    side = fixed(rows, lanes)
    mix_sides = fixed(pages, rows, lanes)

    zlo, zhi, xlo, xhi, ylo, yhi = pack_swap(gas_state, solids_temp, pages, 0)
    flat = gas_state.reshape(count + 1, depth * rows, lanes)
    gas_next, mix, mx_first, mx_last, my_pair = pl.pallas_call(
        species_kernel,
        grid=(steps,),
        out_shape=[shape(count + 1, depth, rows, lanes), shape(depth, rows, lanes)]
        + [shape(depth, lanes)] * 2
        + [shape(pages, rows, lanes)],
        in_specs=[
            pl.BlockSpec((count, CHUNK * rows, lanes), lambda i: (0, i, 0)),
            pl.BlockSpec((count, rows, lanes), lambda i: (0, jnp.maximum(i * CHUNK - 1, 0), 0)),
            pl.BlockSpec((count, rows, lanes), lambda i: (0, jnp.minimum((i + 1) * CHUNK, depth - 1), 0)),
            tops, tops, edges, edges, sides, sides],
        out_specs=[stack(count, 0), planes, edge, edge, mix_sides],
        compiler_params=params(),
    )(flat, flat, flat, zlo, zhi, xlo, xhi, ylo, yhi)
    mix_halos = swap(mix, mx_first, mx_last, my_pair, 1)
    mix_below = pl.BlockSpec((1, rows, lanes), lambda i: (jnp.maximum(i * CHUNK - 1, 0), 0, 0))
    mix_above = pl.BlockSpec((1, rows, lanes), lambda i: (jnp.minimum((i + 1) * CHUNK, depth - 1), 0, 0))
    gas_next, local, ends = pl.pallas_call(
        energy_kernel,
        grid=(steps,),
        out_shape=[
            shape(count + 1, depth, rows, lanes),
            shape(depth * rows, lanes),
            shape(2 * rows + 8, lanes),
        ],
        in_specs=[
            stack(2, 0), stack(1, count), below_of(1, count), above_of(1, count),
            planes, mix_below, mix_above, planes, side, side,
            fixed(*block_inverse.shape), fixed(*line_coupling.shape),
            tops, tops, edges, edges, sides, sides,
            side, side, edge, edge, mix_sides, mix_sides, ANY,
        ],
        out_specs=[stack(1, count), fixed(depth * rows, lanes), fixed(2 * rows + 8, lanes)],
        scratch_shapes=[pltpu.VMEM((depth * rows, lanes), F32)],
        input_output_aliases={24: 0},
        compiler_params=params(),
    )(
        gas_state, gas_state, gas_state, gas_state, mix, mix, mix, solids_temp, exchange_rate, column_flags,
        block_inverse, line_coupling, zlo, zhi, xlo, xhi, ylo, yhi, *mix_halos, gas_next,
    )
    slots = pl.pallas_call(
        share_kernel,
        out_shape=shape(segments, 2 * rows + 8, lanes),
        in_specs=[ANY],
        out_specs=ANY,
        scratch_shapes=[pltpu.SemaphoreType.DMA(()), pltpu.SemaphoreType.DMA((segments,)), pltpu.SemaphoreType.DMA((segments,))],
        compiler_params=pltpu.CompilerParams(collective_id=2, has_side_effects=True, vmem_limit_bytes=63 * 1024 * 1024),
    )(ends)
    part = 2 * CHUNK
    solved = pl.pallas_call(
        finish_kernel,
        out_shape=shape(depth * rows, lanes),
        grid=(depth // part,),
        in_specs=[
            fixed(segments, 2 * rows + 8, lanes),
            pl.BlockSpec((part * rows, lanes), lambda i: (i, 0)),
            pl.BlockSpec((part, depth), lambda i: (i, 0)),
        ],
        out_specs=pl.BlockSpec((part * rows, lanes), lambda i: (i, 0)),
        compiler_params=params(),
    )(slots, local, block_inverse)
    return (gas_next, solved.reshape(depth, rows, lanes))


def solution(mesh):
    in_specs = (
        P(None, "seg", "gx", "gy"),
        P("seg", "gx", "gy"),
        P("gx", "gy"),
        P("gx", "gy"),
        P("seg", None),
        P("seg", None),
    )
    out_specs = (P(None, "seg", "gx", "gy"), P("seg", "gx", "gy"))
    return jax.shard_map(body, mesh=mesh, in_specs=in_specs, out_specs=out_specs, check_vma=False)
```

```python
import jax
import jax.numpy as jnp
from jax import lax
from jax.experimental import pallas as pl
from jax.experimental.pallas import tpu as pltpu
from jax.sharding import PartitionSpec as P

diffusion = (0.1, 0.08, 0.12, 0.09, 0.11, 0.07)
stoich = (-1.0, -0.5, 1.0, 0.5, 0.25, 0.75)
rate_const = 0.3
upwind = 0.25
cond_base = 0.04
cond_slope = 0.3
heat_release = 0.5
lateral = 0.1
loss_table = (0.0, 0.3, 0.0, 0.1)
feed_table = (0.0, 0.0, 0.4, 0.0)
highest = lax.Precision.HIGHEST


MESH = pl.DeviceIdType.MESH
ANY = pl.BlockSpec(memory_space=pl.ANY)
F32 = jnp.float32
CHUNK = 16


def shape(*dims):
    return jax.ShapeDtypeStruct(dims, F32)


def params():
    return pltpu.CompilerParams(vmem_limit_bytes=63 * 1024 * 1024)


def iotas(rows, lanes):
    row = lax.broadcasted_iota(jnp.int32, (rows, lanes), 0)
    lane = lax.broadcasted_iota(jnp.int32, (rows, lanes), 1)
    return row, lane


def pack_columns(packed, plane, k, lane):
    lanes = plane.shape[1]
    moved = pltpu.roll(plane, 2 * k, 1) if k else plane
    ours = (lane == 2 * k) | (lane == (2 * k - 1) % lanes)
    return jnp.where(ours, moved, packed)


def page_of(step, lanes):
    per_page = lanes // (2 * CHUNK)
    return step // per_page, lax.rem(step, per_page) * (2 * CHUNK)


def merge_pages(low, high, lane):
    lanes = low.shape[1]
    return jnp.where(lane % 2 == 0, pltpu.roll(low, 1, 1), pltpu.roll(high, lanes - 1, 1))


def chunk_halo(low, high, step, lane):
    lanes = low.shape[1]
    _, offset = page_of(step, lanes)
    return pltpu.roll(merge_pages(low, high, lane), lax.rem(lanes - offset, lanes), 1)


def shifted(plane, row, lane, k, xlo, xhi, halo, less=None, more=None):
    rows, lanes = plane.shape
    less = pltpu.roll(plane, 1, 0) if less is None else less
    more = pltpu.roll(plane, rows - 1, 0) if more is None else more
    west = jnp.where(row == 0, xlo, less)
    east = jnp.where(row == rows - 1, xhi, more)
    column = pltpu.roll(halo, lanes - 2 * k, 1) if k else halo
    south = jnp.where(lane == 0, column, pltpu.roll(plane, 1, 1))
    north = jnp.where(lane == lanes - 1, column, pltpu.roll(plane, lanes - 1, 1))
    return west, east, south, north


def pack_field(held, field, chunk, x_first, x_last, y_pair):
    rows, lanes = y_pair.shape[2:]
    _, lane = iotas(rows, lanes)
    packed = jnp.zeros((rows, lanes), F32)
    for k in range(CHUNK):
        z = chunk * CHUNK + k
        packed = pack_columns(packed, held[pl.ds(z * rows, rows), :], k, lane)
    start, span = chunk * CHUNK, pl.ds(chunk * CHUNK, CHUNK)
    x_first[field, span] = held[pl.ds(start * rows, CHUNK, stride=rows), :]
    x_last[field, span] = held[pl.ds(start * rows + rows - 1, CHUNK, stride=rows), :]
    per_page = lanes // (2 * CHUNK)
    page, offset = chunk // per_page, chunk % per_page * (2 * CHUNK)
    moved = pltpu.roll(packed, offset, 1) if offset else packed
    y_pair[page, field] = moved if offset == 0 else y_pair[page, field] + moved


def pack_swap_kernel(
    gas, temp, zlo, zhi, xlo, xhi, ylo, yhi,
    gas_held, temp_held, x_first, x_last, y_pair, x_blank, z_blank, y_blank, load_sem, zero_sem, send_sem, recv_sem,
):
    fields, depth, rows = gas.shape[0], x_first.shape[1], y_pair.shape[2]
    loads = []
    for chunk in range(depth // CHUNK):
        span = pl.ds(chunk * CHUNK * rows, CHUNK * rows)
        loads.append(
            (
                pltpu.make_async_copy(gas.at[:, span], gas_held.at[:, span], load_sem.at[2 * chunk]),
                pltpu.make_async_copy(temp.at[span], temp_held.at[span], load_sem.at[2 * chunk + 1]),
            )
        )
    for pair in loads:
        for load in pair:
            load.start()

    def prepare():
        for chunk, pair in enumerate(loads):
            for load in pair:
                load.wait()

            def one(field, carry, chunk=chunk):
                pack_field(gas_held.at[field], field, chunk, x_first, x_last, y_pair)
                return carry

            lax.fori_loop(0, fields, one, 0)
            pack_field(temp_held, fields, chunk, x_first, x_last, y_pair)

    swap_faces(
        (
            ("gx", x_first, x_last, xlo, xhi),
            ("seg", gas.at[:, pl.ds(0, rows)], gas.at[:, pl.ds((depth - 1) * rows, rows)], zlo, zhi),
            ("gy", y_pair, y_pair, ylo, yhi),
        ),
        (x_blank, z_blank, y_blank),
        zero_sem,
        send_sem,
        recv_sem,
        prepare,
    )


def pack_swap(gas, temp, pages, ident):
    fields = gas.shape[0] + 1
    depth, rows, lanes = temp.shape
    top = shape(gas.shape[0], rows, lanes)
    side = shape(fields, depth, lanes)
    edge = shape(pages, fields, rows, lanes)
    sems = pltpu.SemaphoreType.DMA((6,))
    flat_gas = gas.reshape(gas.shape[0], depth * rows, lanes)
    flat_temp = temp.reshape(depth * rows, lanes)
    return pl.pallas_call(
        pack_swap_kernel,
        out_shape=[top, top, side, side, edge, edge],
        in_specs=[ANY] * 2,
        out_specs=[ANY] * 6,
        scratch_shapes=[
            pltpu.VMEM(held.shape, F32) for held in (flat_gas, flat_temp, side, side, edge, side, top, edge)
        ]
        + [pltpu.SemaphoreType.DMA((2 * (depth // CHUNK),)), sems, sems, sems],
        compiler_params=pltpu.CompilerParams(collective_id=ident, has_side_effects=True, vmem_limit_bytes=63 * 1024 * 1024),
    )(flat_gas, flat_temp)


def swap_faces(axes, blanks, zero_sem, send_sem, recv_sem, prepare=None):
    barrier = pltpu.get_barrier_semaphore()
    places = []
    for name, *_ in axes:
        here, count = lax.axis_index(name), lax.axis_size(name)
        places.append((here, here > 0, here < count - 1))
    for (name, *_), (here, down, up) in zip(axes, places):
        for exists, step in ((down, -1), (up, 1)):

            @pl.when(exists)
            def _(name=name, here=here, step=step):
                pl.semaphore_signal(barrier, inc=1, device_id={name: here + step}, device_id_type=MESH)

    peers = sum(exists.astype(jnp.int32) for _, *both in places for exists in both)
    pl.semaphore_wait(barrier, peers)

    plan = []
    for index, ((name, first, last, low, high), (here, down, up)) in enumerate(zip(axes, places)):
        to_up = pltpu.make_async_remote_copy(
            src_ref=last, dst_ref=low, send_sem=send_sem.at[2 * index], recv_sem=recv_sem.at[2 * index],
            device_id={name: here + 1}, device_id_type=MESH)
        to_down = pltpu.make_async_remote_copy(
            src_ref=first, dst_ref=high, send_sem=send_sem.at[2 * index + 1], recv_sem=recv_sem.at[2 * index + 1],
            device_id={name: here - 1}, device_id_type=MESH)
        plan.append((to_up, to_down, down, up, low, high))
    early = [entry for entry, axis in zip(plan, axes) if prepare is None or axis[0] == "seg"]
    for to_up, to_down, down, up, _, _ in early:
        pl.when(up)(to_up.start)
        pl.when(down)(to_down.start)
    for blank in blanks:
        blank[...] = jnp.zeros(blank.shape, F32)
    fills = []
    for index, (_, _, down, up, low, high) in enumerate(plan):
        for side, (exists, halo) in enumerate(((down, low), (up, high))):
            fill = pltpu.make_async_copy(blanks[index], halo, zero_sem.at[2 * index + side])
            fills.append((jnp.logical_not(exists), fill))
    for missing, fill in fills:
        pl.when(missing)(fill.start)
    if prepare is not None:
        prepare()
        for (to_up, to_down, down, up, _, _), axis in zip(plan, axes):
            if axis[0] != "seg":
                pl.when(up)(to_up.start)
                pl.when(down)(to_down.start)
    for to_up, to_down, down, up, low, high in plan:
        pl.when(up)(to_up.wait_send)
        pl.when(down)(to_down.wait_send)
        pl.when(down)(to_up.wait_recv)
        pl.when(up)(to_down.wait_recv)
    for missing, fill in fills:
        pl.when(missing)(fill.wait)


def swap_kernel(
    field, x_first, x_last, y_pair, zlo, zhi, xlo, xhi, ylo, yhi, x_blank, z_blank, y_blank, zero_sem, send_sem, recv_sem
):
    if len(field.shape) == 4:
        z_first, z_last = field.at[:, 0], field.at[:, field.shape[1] - 1]
    else:
        z_first, z_last = field.at[0], field.at[field.shape[0] - 1]
    swap_faces(
        (
            ("gx", x_first, x_last, xlo, xhi),
            ("seg", z_first, z_last, zlo, zhi),
            ("gy", y_pair, y_pair, ylo, yhi),
        ),
        (x_blank, z_blank, y_blank),
        zero_sem,
        send_sem,
        recv_sem,
    )


def swap(field, x_first, x_last, y_pair, ident):
    top = shape(*field.shape[:-3], *field.shape[-2:])
    side = shape(*x_first.shape)
    edge = shape(*y_pair.shape)
    sems = pltpu.SemaphoreType.DMA((6,))
    return pl.pallas_call(
        swap_kernel,
        out_shape=[top, top, side, side, edge, edge],
        in_specs=[ANY] * 4,
        out_specs=[ANY] * 6,
        scratch_shapes=[pltpu.VMEM(face.shape, F32) for face in (side, top, edge)] + [sems, sems, sems],
        compiler_params=pltpu.CompilerParams(collective_id=ident, has_side_effects=True, vmem_limit_bytes=63 * 1024 * 1024),
    )(field, x_first, x_last, y_pair)


def species_kernel(
    gas, before, after, zlo, zhi, xlo, xhi, ylo, yhi, new, mix_out, x_first, x_last, y_pair
):
    step, steps = pl.program_id(0), pl.num_programs(0)
    count, depth, rows, lanes = new.shape
    row, lane = iotas(rows, lanes)
    at_bottom, at_top = step == 0, step == steps - 1

    @pl.when(step == 0)
    def _():
        y_pair[...] = jnp.zeros_like(y_pair)

    page, offset = page_of(step, lanes)
    packed = jnp.zeros((rows, lanes), F32)
    halos = [chunk_halo(ylo[page, s], yhi[page, s], step, lane) for s in range(count)]
    for k in range(depth):
        here = slice(k * rows, (k + 1) * rows)
        reaction = rate_const * gas[0, here] * gas[1, here]
        total = None
        for s in range(count):
            center = gas[s, here]
            down, up = slice((k - 1) * rows, k * rows), slice((k + 1) * rows, (k + 2) * rows)
            below = gas[s, down] if k > 0 else jnp.where(at_bottom, zlo[s], before[s])
            above = gas[s, up] if k < depth - 1 else jnp.where(at_top, zhi[s], after[s])
            less = gas[s, k * rows - 1 : (k + 1) * rows - 1] if k > 0 else None
            more = gas[s, k * rows + 1 : (k + 1) * rows + 1] if k < depth - 1 else None
            west, east, south, north = shifted(
                center, row, lane, k, xlo[s, k : k + 1], xhi[s, k : k + 1], halos[s], less, more
            )
            beside = (below + above) + (west + east) + (south + north)
            value = (
                center
                + diffusion[s] * (beside - 6.0 * center)
                - upwind * (center - below)
                + stoich[s] * reaction
            )
            new[s, k] = value
            total = value if total is None else total + value
        mix = 0.5 * total
        mix_out[k] = mix
        packed = pack_columns(packed, mix, k, lane)
        x_first[k : k + 1] = mix[0:1]
        x_last[k : k + 1] = mix[rows - 1 : rows]
    y_pair[page] += pltpu.roll(packed, offset, 1)


def lookup(flags, table):
    result = jnp.zeros(flags.shape, F32)
    for value, entry in enumerate(table):
        result = result + jnp.where(flags == value, entry, 0.0)
    return result


def energy_kernel(
    pair, heat, heat_before, heat_after, mix, mix_before, mix_after, temp, exchange, flags, inverse, coupling,
    zlo, zhi, xlo, xhi, ylo, yhi, mzlo, mzhi, mxlo, mxhi, mylo, myhi, gas_in,
    heat_out, local, ends, source,
):
    step, steps = pl.program_id(0), pl.num_programs(0)
    depth, rows, lanes = temp.shape
    row, lane = iotas(rows, lanes)
    at_bottom, at_top = step == 0, step == steps - 1
    loss = lookup(flags[...], loss_table)
    feed = lookup(flags[...], feed_table)
    rate = exchange[...]
    page, _ = page_of(step, lanes)
    heat_halo = chunk_halo(ylo[page, 0], yhi[page, 0], step, lane)
    temp_halo = chunk_halo(ylo[page, 1], yhi[page, 1], step, lane)
    mix_halo = chunk_halo(mylo[page], myhi[page], step, lane)
    for k in range(depth):
        z = step * depth + k
        reaction = rate_const * pair[0, k] * pair[1, k]
        heat_mid, mix_mid, temp_mid = heat[0, k], mix[k], temp[k]
        heat_below = heat[0, k - 1] if k > 0 else jnp.where(at_bottom, zlo[0], heat_before[0, 0])
        heat_above = heat[0, k + 1] if k < depth - 1 else jnp.where(at_top, zhi[0], heat_after[0, 0])
        mix_below = mix[k - 1] if k > 0 else jnp.where(at_bottom, mzlo[...], mix_before[0])
        mix_above = mix[k + 1] if k < depth - 1 else jnp.where(at_top, mzhi[...], mix_after[0])
        one = slice(k, k + 1)
        heats = (heat_below, heat_above) + shifted(
            heat_mid, row, lane, k, xlo[0, one], xhi[0, one], heat_halo
        )
        mixes = (mix_below, mix_above) + shifted(
            mix_mid, row, lane, k, mxlo[one], mxhi[one], mix_halo
        )
        temps = shifted(temp_mid, row, lane, k, xlo[1, one], xhi[1, one], temp_halo)
        cond_mid = cond_base + cond_slope * mix_mid
        flux = None
        for heat_near, mix_near in zip(heats, mixes):
            part = (cond_mid + (cond_base + cond_slope * mix_near)) * (heat_near - heat_mid)
            flux = part if flux is None else flux + part
        heat_new = heat_mid + 0.5 * flux + heat_release * reaction - loss * heat_mid + feed
        heat_out[0, k] = heat_new
        beside = (temps[0] + temps[1]) + (temps[2] + temps[3])
        planes = temp_mid + lateral * (beside - 4.0 * temp_mid) + rate * (heat_new - temp_mid)
        source[pl.ds(pl.multiple_of(z * rows, rows), rows), :] = planes

    @pl.when(at_top)
    def _():
        size = inverse.shape[0]
        group = 4
        for start in range(0, rows, group):
            right = jnp.concatenate(
                [source[pl.ds(start + j, size, stride=rows), :] for j in range(group)], axis=1
            )
            result = jnp.dot(inverse[...], right, precision=highest, preferred_element_type=F32)
            for j in range(group):
                local[pl.ds(start + j, size, stride=rows), :] = result[:, j * lanes : (j + 1) * lanes]
        ends[0:rows] = local[0:rows]
        ends[rows : 2 * rows] = local[(size - 1) * rows : size * rows]
        scalars = (
            inverse[0:1, 0:1],
            inverse[size - 1 : size, 0:1],
            inverse[0:1, size - 1 : size],
            inverse[size - 1 : size, size - 1 : size],
            coupling[0:1, 0:1],
            coupling[0:1, 1:2],
        )
        for index, scalar in enumerate(scalars):
            ends[2 * rows + index : 2 * rows + index + 1] = jnp.broadcast_to(scalar, (1, lanes))
        ends[2 * rows + 6 : 2 * rows + 8] = jnp.zeros((2, lanes), F32)


def share_kernel(ends, slots, own_sem, send_sem, recv_sem):
    here, count = lax.axis_index("seg"), lax.axis_size("seg")
    barrier = pltpu.get_barrier_semaphore()
    for step in range(1, count):
        pl.semaphore_signal(
            barrier, inc=1, device_id={"seg": lax.rem(here + step, count)}, device_id_type=MESH)
    pl.semaphore_wait(barrier, count - 1)
    copies = [
        pltpu.make_async_remote_copy(
            src_ref=ends, dst_ref=slots.at[step], send_sem=send_sem.at[step], recv_sem=recv_sem.at[step],
            device_id={"seg": lax.rem(here + step, count)}, device_id_type=MESH)
        for step in range(1, count)
    ]
    for copy in copies:
        copy.start()
    own = pltpu.make_async_copy(ends, slots.at[0], own_sem)
    own.start()
    own.wait()
    for copy in copies:
        copy.wait()


def finish_kernel(slots, local, inverse, out):
    count, total_rows, lanes = slots.shape
    rows = (total_rows - 8) // 2
    size, width = inverse.shape
    here = lax.axis_index("seg")
    held = [slots[lax.rem(here - s + count, count)] for s in range(count)]
    p_lines, q_lines = [], []
    for s in range(count):
        y_first, y_last = held[s][0:rows], held[s][rows : 2 * rows]
        b00, b90, b09, b99, lower, upper = (held[s][2 * rows + j : 2 * rows + j + 1] for j in range(6))
        p_gain = upper * b09 if s < count - 1 else jnp.zeros_like(upper)
        q_gain = upper * b99 if s < count - 1 else jnp.zeros_like(upper)
        p_const, q_const = y_first, y_last
        if s > 0:
            before_const, before_gain = q_lines[-1]
            into_p, into_q = lower * b00, lower * b90
            scale = 1.0 / (1.0 - into_p * before_gain)
            p_const = (y_first + into_p * before_const) * scale
            p_gain = p_gain * scale
            link = into_q * before_gain
            q_const = y_last + into_q * before_const + link * p_const
            q_gain = q_gain + link * p_gain
        p_lines.append((p_const, p_gain))
        q_lines.append((q_const, q_gain))
    firsts, lasts = [None] * count, [None] * count
    above = jnp.zeros((rows, lanes), F32)
    for s in reversed(range(count)):
        firsts[s] = p_lines[s][0] + p_lines[s][1] * above
        lasts[s] = q_lines[s][0] + q_lines[s][1] * above
        above = firsts[s]
    q_near = jnp.zeros((rows, lanes), F32)
    p_near = jnp.zeros((rows, lanes), F32)
    for s in range(count):
        if s > 0:
            q_near = jnp.where(here == s, lasts[s - 1], q_near)
        if s < count - 1:
            p_near = jnp.where(here == s, firsts[s + 1], p_near)
    mine = slots[0]
    q_near = mine[2 * rows + 4 : 2 * rows + 5] * q_near
    p_near = mine[2 * rows + 5 : 2 * rows + 6] * p_near
    for z in range(size):
        low = jnp.broadcast_to(inverse[z : z + 1, 0:1], (1, lanes))
        high = jnp.broadcast_to(inverse[z : z + 1, width - 1 : width], (1, lanes))
        block = slice(z * rows, (z + 1) * rows)
        out[block] = local[block] + q_near * low + p_near * high


def body(gas_state, solids_temp, exchange_rate, column_flags, block_inverse, line_coupling):
    count = gas_state.shape[0] - 1
    depth, rows, lanes = solids_temp.shape
    segments = lax.axis_size("seg")
    steps = depth // CHUNK

    def fixed(*dims):
        return pl.BlockSpec(dims, lambda i: (0,) * len(dims))

    def stack(number, start):
        return pl.BlockSpec((number, CHUNK, rows, lanes), lambda i: (start, i, 0, 0))

    def below_of(number, start):
        return pl.BlockSpec(
            (number, 1, rows, lanes), lambda i: (start, jnp.maximum(i * CHUNK - 1, 0), 0, 0))

    def above_of(number, start):
        return pl.BlockSpec(
            (number, 1, rows, lanes), lambda i: (start, jnp.minimum((i + 1) * CHUNK, depth - 1), 0, 0))

    planes = pl.BlockSpec((CHUNK, rows, lanes), lambda i: (i, 0, 0))
    edge = pl.BlockSpec((CHUNK, lanes), lambda i: (i, 0))
    edges = pl.BlockSpec((count, CHUNK, lanes), lambda i: (0, i, 0))
    last_edges = pl.BlockSpec((2, CHUNK, lanes), lambda i: (count // 2, i, 0))
    last_top = pl.BlockSpec((1, rows, lanes), lambda i: (count, 0, 0))
    pages = -(-2 * depth // lanes)
    sides = fixed(pages, count, rows, lanes)
    last_sides = pl.BlockSpec((pages, 2, rows, lanes), lambda i: (0, count // 2, 0, 0))
    tops = fixed(count, rows, lanes)
    side = fixed(rows, lanes)
    mix_sides = fixed(pages, rows, lanes)

    zlo, zhi, xlo, xhi, ylo, yhi = pack_swap(gas_state, solids_temp, pages, 0)
    flat = gas_state.reshape(count + 1, depth * rows, lanes)
    gas_next, mix, mx_first, mx_last, my_pair = pl.pallas_call(
        species_kernel,
        grid=(steps,),
        out_shape=[shape(count + 1, depth, rows, lanes), shape(depth, rows, lanes)]
        + [shape(depth, lanes)] * 2
        + [shape(pages, rows, lanes)],
        in_specs=[
            pl.BlockSpec((count, CHUNK * rows, lanes), lambda i: (0, i, 0)),
            pl.BlockSpec((count, rows, lanes), lambda i: (0, jnp.maximum(i * CHUNK - 1, 0), 0)),
            pl.BlockSpec((count, rows, lanes), lambda i: (0, jnp.minimum((i + 1) * CHUNK, depth - 1), 0)),
            tops, tops, edges, edges, sides, sides],
        out_specs=[stack(count, 0), planes, edge, edge, mix_sides],
        compiler_params=params(),
    )(flat, flat, flat, zlo, zhi, xlo, xhi, ylo, yhi)
    mix_halos = swap(mix, mx_first, mx_last, my_pair, 1)
    mix_below = pl.BlockSpec((1, rows, lanes), lambda i: (jnp.maximum(i * CHUNK - 1, 0), 0, 0))
    mix_above = pl.BlockSpec((1, rows, lanes), lambda i: (jnp.minimum((i + 1) * CHUNK, depth - 1), 0, 0))
    gas_next, local, ends = pl.pallas_call(
        energy_kernel,
        grid=(steps,),
        out_shape=[
            shape(count + 1, depth, rows, lanes),
            shape(depth * rows, lanes),
            shape(2 * rows + 8, lanes),
        ],
        in_specs=[
            stack(2, 0), stack(1, count), below_of(1, count), above_of(1, count),
            planes, mix_below, mix_above, planes, side, side,
            fixed(*block_inverse.shape), fixed(*line_coupling.shape),
            last_top, last_top, last_edges, last_edges, last_sides, last_sides,
            side, side, edge, edge, mix_sides, mix_sides, ANY,
        ],
        out_specs=[stack(1, count), fixed(depth * rows, lanes), fixed(2 * rows + 8, lanes)],
        scratch_shapes=[pltpu.VMEM((depth * rows, lanes), F32)],
        input_output_aliases={24: 0},
        compiler_params=params(),
    )(
        gas_state, gas_state, gas_state, gas_state, mix, mix, mix, solids_temp, exchange_rate, column_flags,
        block_inverse, line_coupling, zlo, zhi, xlo, xhi, ylo, yhi, *mix_halos, gas_next,
    )
    slots = pl.pallas_call(
        share_kernel,
        out_shape=shape(segments, 2 * rows + 8, lanes),
        in_specs=[ANY],
        out_specs=ANY,
        scratch_shapes=[pltpu.SemaphoreType.DMA(()), pltpu.SemaphoreType.DMA((segments,)), pltpu.SemaphoreType.DMA((segments,))],
        compiler_params=pltpu.CompilerParams(collective_id=2, has_side_effects=True, vmem_limit_bytes=63 * 1024 * 1024),
    )(ends)
    part = 2 * CHUNK
    solved = pl.pallas_call(
        finish_kernel,
        out_shape=shape(depth * rows, lanes),
        grid=(depth // part,),
        in_specs=[
            fixed(segments, 2 * rows + 8, lanes),
            pl.BlockSpec((part * rows, lanes), lambda i: (i, 0)),
            pl.BlockSpec((part, depth), lambda i: (i, 0)),
        ],
        out_specs=pl.BlockSpec((part * rows, lanes), lambda i: (i, 0)),
        compiler_params=params(),
    )(slots, local, block_inverse)
    return (gas_next, solved.reshape(depth, rows, lanes))


def solution(mesh):
    in_specs = (
        P(None, "seg", "gx", "gy"),
        P("seg", "gx", "gy"),
        P("gx", "gy"),
        P("gx", "gy"),
        P("seg", None),
        P("seg", None),
    )
    out_specs = (P(None, "seg", "gx", "gy"), P("seg", "gx", "gy"))
    return jax.shard_map(body, mesh=mesh, in_specs=in_specs, out_specs=out_specs, check_vma=False)
```
